32 devices in a mesh: beam: 2 (over x), freq: 16 (over z, y, core).
Axes of the slice: x: 2, y: 2, z: 4, core: 2. Of those that a mesh axis runs over, the one named last changes fastest.
Arguments:
- spectra: float32 [512, 8192], P(('beam', 'freq')), parts along dimension 0, may hold values from -36 to 36
- profiles: bfloat16 [64, 256], replicated, may hold values from -0.375 to 0.375
- shifts: int32 [15, 32], replicated, may hold values from 0 to 512
Outputs:
- peaks: bfloat16 [512, 64, 64], P(('beam', 'freq')), parts along dimension 0
The draws below stay inside these ranges and needn't reach their ends.
There are 2 independent parts, one for each index of `beam`. The reference program is written for one: setup_inputs(seed, part) draws one part's arguments, and reference() takes and returns one part's arrays. A program takes and returns all parts, laid end to end along the dimension named above; an argument that names none is the same for every part. Nothing has to cross between parts.
All inputs are finite; a program needn't handle non-finite values.
Results may differ from the reference program's by a relative error of at most 0.0048.
Values sent between devices are 32-bit elements; how exact they have to be, the bound alone decides.
No kernel may reach another device: no remote copies, remote signals or barrier semaphores. Data moves between devices by JAX's collectives and lax.ppermute only.
A program may use at most 64 MiB of HBM per device.

```python
import jax
import jax.numpy as jnp
from jax import lax

R = 16
TIME = 8192
PROFS = 64
TAPS = 256
STRIDE = 8
HOLD = 16
SUBBANDS = 16
MAXSHIFT = 512
PEAKS = 64


def draw_spectra(key, part):
    key_base = jax.random.fold_in(key, 11)
    key_gain = jax.random.fold_in(key, 23)
    row_total = SUBBANDS * R
    band_pos = jnp.arange(SUBBANDS, dtype=jnp.float32) / max(SUBBANDS - 1, 1)
    band_scale = 3.0 ** band_pos * jax.random.uniform(key_gain, (SUBBANDS,), jnp.float32, 1.0, 2.0)
    base_draw = jnp.clip(jax.random.normal(key_base, (row_total, TIME), jnp.float32), -6.0, 6.0)
    return (jnp.repeat(band_scale, R)[:, None] * base_draw).astype(jnp.float32)


def set_ends(entries, stream_key, least, largest):
    dims = entries.shape
    place = [jax.random.randint(jax.random.fold_in(stream_key, axis), (), 0, dims[axis]) for axis in range(len(dims))]
    entries = entries.at[tuple(place)].set(least)
    longest = dims.index(max(dims))
    place[longest] = (place[longest] + 1) % dims[longest]
    return entries.at[tuple(place)].set(largest)


def scatter_about(rng, extent, deviation, limit, held_as=jnp.bfloat16):
    array = deviation * jax.random.normal(rng, extent, jnp.float32)
    return jnp.clip(array, min=-limit, max=limit).astype(held_as)


def setup_inputs(seed: int = 0, part: int = 0) -> dict:
    streams_of = jax.random.split(jax.random.key(seed), 4)
    part_keys = jax.random.split(jax.random.fold_in(streams_of[3], part), 4)
    spectra = draw_spectra(jax.random.fold_in(jax.random.fold_in(streams_of[3], part), 71), part)
    profiles = scatter_about(streams_of[1], (PROFS, TAPS), TAPS ** -0.5, 0.375)
    shifts = set_ends(jax.random.randint(streams_of[2], (SUBBANDS - 1, 2 * R), 0, MAXSHIFT + 1), jax.random.fold_in(streams_of[2], 1), 0, MAXSHIFT).astype(jnp.int32)
    return dict(spectra=spectra, profiles=profiles, shifts=shifts)


def merge_level(current, shifts, tree_level):
    subband_count, row_count, time_len = current.shape
    device_index = jnp.arange(subband_count, dtype=jnp.int32)
    upper_bit = device_index >> tree_level & 1
    low_index = device_index - upper_bit * (1 << tree_level)
    high_index = low_index + (1 << tree_level)
    tree_node = subband_count - (subband_count >> tree_level) + (device_index >> tree_level + 1)
    merged_row = upper_bit[:, None] * row_count + jnp.arange(row_count, dtype=jnp.int32)[None, :]
    source_row = merged_row // 2
    delays = shifts[tree_node[:, None], merged_row]
    low_rows = current[low_index[:, None], source_row]
    high_rows = current[high_index[:, None], source_row]
    source_time = jnp.arange(time_len, dtype=jnp.int32)[None, None, :] - delays[:, :, None]
    shifted = jnp.take_along_axis(high_rows, jnp.maximum(source_time, 0), axis=2)
    return low_rows + jnp.where(source_time >= 0, shifted, jnp.zeros_like(shifted))

def correlate(rows_bf, profiles, rms_level):
    row_count, time_len = rows_bf.shape
    tap_count = profiles.shape[1]
    positions = time_len // STRIDE
    padded = jnp.pad(rows_bf, ((0, 0), (0, tap_count)))
    frames = padded.reshape(row_count, (time_len + tap_count) // STRIDE, STRIDE)
    windows = jnp.concatenate([frames[:, lag_index:lag_index + positions] for lag_index in range(tap_count // STRIDE)], axis=2)
    products = jnp.einsum('npq,kq->nkp', windows.astype(jnp.float32), profiles.astype(jnp.float32))
    scaled = products / rms_level
    return lax.optimization_barrier(jnp.max(scaled.reshape(row_count, profiles.shape[0], positions // HOLD, HOLD), axis=3)).astype(jnp.bfloat16)

def reference(spectra, profiles, shifts):
    level_count = SUBBANDS.bit_length() - 1
    rms_level = jnp.sqrt(SUBBANDS * jnp.sum(spectra * spectra) / (SUBBANDS * R * TIME) + 1e-06)
    current = spectra.reshape(SUBBANDS, R, TIME)
    for tree_level in range(level_count):
        current = merge_level(current, shifts, tree_level)
    rows_bf = current.astype(jnp.bfloat16)
    peaks_all = lax.map(lambda row_block: correlate(row_block, profiles, rms_level), rows_bf)
    return peaks_all.reshape(SUBBANDS * R, PROFS, PEAKS)
```

```python
import functools

import jax
import jax.numpy as jnp
from jax import lax
from jax.experimental import pallas as pl
from jax.experimental.pallas import tpu as pltpu
from jax.sharding import PartitionSpec as P

STRIDE = 8
HOLD = 16
LANES = 128
HALO = 8
VMEM_LIMIT = 48 * 1024 * 1024


def reversed_bits(value, count):
    result = 0
    for bit in range(count):
        result |= ((value >> bit) & 1) << (count - 1 - bit)
    return result


def pack_kernel(x_ref, msg_ref):
    row_count, time_len = x_ref.shape
    block_count = time_len // LANES
    stride = block_count + HALO
    power = jnp.zeros((8, LANES), jnp.float32)
    for column in range(block_count):
        for half in range(row_count // 8):
            piece = x_ref[half * 8 : half * 8 + 8, column * LANES : (column + 1) * LANES]
            power = power + piece * piece
            msg_ref[pl.ds(half * 8 * stride + column, 8, stride=stride), :] = piece
    for row in range(row_count):
        msg_ref[row * stride + block_count : (row + 1) * stride, :] = power


def tree_levels(first, second, shifts_ref, index, low_bit, bit_count, subband_count, row_count, block_count):
    row_bits = row_count.bit_length() - 1
    stride = block_count + HALO
    lane = lax.broadcasted_iota(jnp.int32, (block_count, LANES), 1)
    own = [(index >> (low_bit + k)) & 1 for k in range(bit_count)]
    source, target = first, second
    for k in range(bit_count):
        level = low_bit + k
        sources = 1 << (row_bits - bit_count + k)
        base = 0
        for q in range(k + 1, bit_count):
            base = base + (own[q] << (row_bits - 1 - (q - k - 1)))
        column = own[k] * row_count + base
        for group in range(1 << (bit_count - k - 1)):
            node = (
                subband_count
                - (subband_count >> level)
                + ((index >> (low_bit + bit_count)) << (bit_count - k - 1))
                + group
            )
            for row in range(2 * sources):
                if k == 0:
                    low = reversed_bits(2 * group, bit_count) * sources + row // 2
                    high = reversed_bits(2 * group + 1, bit_count) * sources + row // 2
                else:
                    low = 2 * group * sources + row // 2
                    high = low + sources
                delay = shifts_ref[node, column + row]
                lines, part = delay >> 7, delay & (LANES - 1)
                at = high * stride + HALO
                near = source[pl.ds(at - lines, block_count), :]
                far = source[pl.ds(at - lines - 1, block_count), :]
                moved = pltpu.roll(jnp.where(lane < LANES - part, near, far), part, 1)
                kept = source[low * stride + HALO : (low + 1) * stride, :]
                slot = (group * 2 * sources + row) * stride + HALO
                target[slot : slot + block_count, :] = kept + moved
        source, target = target, source
    return source


def unpack(msg_ref, first, second, row_count, block_count, per_message):
    stride = block_count + HALO
    span = per_message * block_count + HALO
    zeros = jnp.zeros((HALO, LANES), jnp.float32)
    power = zeros
    for scratch in (first, second):
        for row in range(row_count + 1):
            scratch[row * stride : row * stride + HALO, :] = zeros
    for message in range(row_count // per_message):
        for part in range(per_message):
            row = message * per_message + part
            first[row * stride + HALO : (row + 1) * stride, :] = msg_ref[
                message * span + part * block_count : message * span + (part + 1) * block_count, :
            ]
        power = power + msg_ref[message * span + per_message * block_count : (message + 1) * span, :]
    return power


def merge_kernel(low_bit, bit_count, next_bits, subband_count, row_count, block_count, shifts_ref, msg_ref, out_ref, first, second):
    index = lax.axis_index("freq")
    stride = block_count + HALO
    power = unpack(msg_ref, first, second, row_count, block_count, row_count >> bit_count)
    final = tree_levels(first, second, shifts_ref, index, low_bit, bit_count, subband_count, row_count, block_count)
    per_message = row_count >> next_bits
    span = per_message * block_count + HALO
    for message in range(1 << next_bits):
        for part in range(per_message):
            row = message * per_message + part
            out_ref[message * span + part * block_count : message * span + (part + 1) * block_count, :] = final[
                row * stride + HALO : (row + 1) * stride, :
            ]
        out_ref[message * span + per_message * block_count : (message + 1) * span, :] = power


def final_kernel(
    low_bit, bit_count, subband_count, row_count, block_count, shifts_ref, prof_ref, msg_ref, out_ref,
    first, second, windows, table,
):
    index = lax.axis_index("freq")
    stride = block_count + HALO
    prof_count, tap_count = prof_ref.shape
    span_len = table.shape[1]
    blocks = span_len // LANES
    power = unpack(msg_ref, first, second, row_count, block_count, row_count >> bit_count)
    profiles = jnp.concatenate(
        [prof_ref[...].astype(jnp.float32), jnp.zeros((prof_count, span_len - tap_count), jnp.float32)], axis=1
    )
    for offset in range(HOLD):
        moved = profiles if offset == 0 else pltpu.roll(profiles, offset * STRIDE, 1)
        table[offset * prof_count : (offset + 1) * prof_count, :] = moved.astype(jnp.bfloat16)
    final = tree_levels(first, second, shifts_ref, index, low_bit, bit_count, subband_count, row_count, block_count)
    for row in range(row_count):
        for block in range(blocks):
            at = row * stride + HALO + block
            windows[row * block_count : (row + 1) * block_count, block * LANES : (block + 1) * LANES] = final[
                at : at + block_count, :
            ].astype(jnp.bfloat16)
    total = jnp.sum(jnp.sum(power, axis=0, keepdims=True), axis=1, keepdims=True)
    samples = subband_count * row_count * block_count * LANES
    rms_level = jnp.sqrt(subband_count * total / samples + 1e-06)
    group = 256 // block_count
    for start in range(0, row_count, group):
        products = lax.dot_general(
            table[...],
            windows[start * block_count : (start + group) * block_count, :],
            (((1,), (1,)), ((), ())),
            preferred_element_type=jnp.float32,
        )
        best = products[:prof_count]
        for offset in range(1, HOLD):
            best = jnp.maximum(best, products[offset * prof_count : (offset + 1) * prof_count])
        best = best / rms_level
        for row in range(group):
            out_ref[start + row] = best[:, row * block_count : (row + 1) * block_count].astype(jnp.bfloat16)


def stage_groups(subband_count, low_bit, bit_count):
    groups = []
    for rest in range(subband_count >> bit_count):
        low = rest & ((1 << low_bit) - 1)
        high = rest >> low_bit
        groups.append(
            [
                low + (reversed_bits(slot, bit_count) << low_bit) + (high << (low_bit + bit_count))
                for slot in range(1 << bit_count)
            ]
        )
    return groups


def per_device(spectra, profiles, shifts):
    row_count, time_len = spectra.shape
    prof_count, tap_count = profiles.shape
    subband_count = lax.axis_size("freq")
    level_count = subband_count.bit_length() - 1
    row_bits = row_count.bit_length() - 1
    block_count = time_len // LANES
    stages = []
    while sum(stages) < level_count:
        stages.append(min(row_bits, level_count - sum(stages)))
    vmem = pl.BlockSpec(memory_space=pltpu.VMEM)
    smem = pl.BlockSpec(memory_space=pltpu.SMEM)
    params = pltpu.CompilerParams(vmem_limit_bytes=VMEM_LIMIT)
    states = [pltpu.VMEM(((row_count + 1) * (block_count + HALO), LANES), jnp.float32)] * 2

    def message_shape(bit_count):
        return jax.ShapeDtypeStruct(((row_count * block_count + (HALO << bit_count)), LANES), jnp.float32)

    messages = pl.pallas_call(
        pack_kernel,
        out_shape=message_shape(stages[0]),
        in_specs=[vmem],
        out_specs=vmem,
        compiler_params=params,
    )(spectra)
    low_bit = 0
    for number, bit_count in enumerate(stages):
        shape = messages.shape
        messages = lax.all_to_all(
            messages.reshape(1 << bit_count, -1, LANES),
            "freq",
            0,
            0,
            tiled=True,
            axis_index_groups=stage_groups(subband_count, low_bit, bit_count),
        ).reshape(shape)
        sizes = (subband_count, row_count, block_count)
        if number + 1 < len(stages):
            next_bits = stages[number + 1]
            messages = pl.pallas_call(
                functools.partial(merge_kernel, low_bit, bit_count, next_bits, *sizes),
                out_shape=message_shape(next_bits),
                in_specs=[smem, vmem],
                out_specs=vmem,
                scratch_shapes=states,
                compiler_params=params,
            )(shifts, messages)
        low_bit += bit_count
    block_len = STRIDE * HOLD
    extra = (tap_count + block_len - STRIDE - 1) // block_len
    span_len = (extra + 1) * block_len
    return pl.pallas_call(
        functools.partial(final_kernel, low_bit - bit_count, bit_count, *sizes),
        out_shape=jax.ShapeDtypeStruct((row_count, prof_count, block_count), jnp.bfloat16),
        in_specs=[smem, vmem, vmem],
        out_specs=vmem,
        scratch_shapes=states
        + [
            pltpu.VMEM((row_count * block_count, span_len), jnp.bfloat16),
            pltpu.VMEM((HOLD * prof_count, span_len), jnp.bfloat16),
        ],
        compiler_params=params,
    )(shifts, profiles, messages)


def solution(mesh):
    in_specs = (P(("beam", "freq"), None), P(), P())
    out_specs = P(("beam", "freq"), None, None)
    return jax.shard_map(
        per_device, mesh=mesh, in_specs=in_specs, out_specs=out_specs, check_vma=False
    )
```

```python
import functools
import itertools

import jax
import jax.numpy as jnp
from jax import lax
from jax.experimental import pallas as pl
from jax.experimental.pallas import tpu as pltpu
from jax.sharding import PartitionSpec as P

STRIDE = 8
HOLD = 16
LANES = 128
HALO = 8
VMEM_LIMIT = 48 * 1024 * 1024
RAW_MASKS = (4, 5)
MERGED_MASKS = (6, 7, 2, 3, 1)


def reversed_bits(value, count):
    result = 0
    for bit in range(count):
        result |= ((value >> bit) & 1) << (count - 1 - bit)
    return result


def lines_at(start, count):
    return pl.ds(pl.multiple_of(start, 8), count)


def pack_rows(x_ref, store):
    row_count, time_len = x_ref.shape
    power = jnp.zeros((8, LANES), jnp.float32)
    for column in range(time_len // LANES):
        for half in range(row_count // 8):
            piece = x_ref[half * 8 : half * 8 + 8, column * LANES : (column + 1) * LANES]
            power = power + piece * piece
            store(half, column, piece)
    return power


def pack_kernel(x_ref, msg_ref):
    row_count, time_len = x_ref.shape
    block_count = time_len // LANES
    stride = HALO + block_count

    def store(half, column, piece):
        msg_ref[pl.ds(half * 8 * stride + HALO + column, 8, stride=stride), :] = piece

    power = pack_rows(x_ref, store)
    for row in range(row_count):
        msg_ref[row * stride : row * stride + HALO, :] = power


def split_kernel(x_ref, *refs):
    raw_refs, (sent_ref, kept_ref) = refs[:-2], refs[-2:]
    index = lax.axis_index("freq")
    core, chip = index & 1, (index >> 1) & 7
    row_count, time_len = x_ref.shape
    block_count = time_len // LANES
    half_span = row_count // 2 * block_count

    def body(own_half):
        def store(half, column, piece):
            ref = kept_ref if half == own_half else sent_ref
            ref[pl.ds(HALO + column, 8, stride=block_count), :] = piece

        power = pack_rows(x_ref, store)
        kept_ref[:HALO, :] = power
        sent_ref[:HALO, :] = power
        for number, mask in enumerate(RAW_MASKS):
            place = reversed_bits(chip ^ mask, 3)
            for flip, ref in enumerate((kept_ref, sent_ref)):
                out_ref = raw_refs[2 * number + flip]
                out_ref[HALO:, :] = ref[lines_at(HALO + place * block_count, block_count), :]
                out_ref[:HALO, :] = power

    for own_half in range(2):
        pl.when(core == own_half)(functools.partial(body, own_half))


def delayed(source, high, delay, block_count):
    lane = lax.broadcasted_iota(jnp.int32, (block_count, LANES), 1)
    line = lax.broadcasted_iota(jnp.int32, (HALO, LANES), 0)
    lines, part = delay >> 7, delay & (LANES - 1)
    near = source[pl.ds(high - lines, block_count), :]
    far = source[pl.ds(high - lines - 1, block_count), :]
    moved = pltpu.roll(jnp.where(lane < LANES - part, near, far), part, 1)
    head = jnp.where(line * LANES + lane[:HALO] >= delay, moved[:HALO], 0.0)
    return jnp.concatenate([head, moved[HALO:]], axis=0)


def core_merge_kernel(block_count, row_count, shifts_ref, got_ref, kept_ref, *outs):
    index = lax.axis_index("freq")
    core, chip = index & 1, (index >> 1) & 7

    def body(low_ref, high_ref):
        power = low_ref[:HALO, :] + high_ref[:HALO, :]
        for mask, out_ref in zip((0,) + MERGED_MASKS, outs):
            place = reversed_bits(chip ^ mask, 3)
            at = HALO + place * block_count
            for part in range(2):
                delay = shifts_ref[index >> 1, core * row_count + 2 * place + part]
                out_ref[HALO + part * block_count : HALO + (part + 1) * block_count, :] = low_ref[
                    lines_at(at, block_count), :
                ] + delayed(high_ref, at, delay, block_count)
            out_ref[:HALO, :] = power

    pl.when(core == 0)(lambda: body(kept_ref, got_ref))
    pl.when(core == 1)(lambda: body(got_ref, kept_ref))


def tree_levels(first, second, shifts_ref, index, low_bit, bit_count, subband_count, row_count, block_count):
    row_bits = row_count.bit_length() - 1
    own = [(index >> (low_bit + k)) & 1 for k in range(bit_count)]
    source, target = first, second
    for k in range(bit_count):
        level = low_bit + k
        sources = 1 << (row_bits - bit_count + k)
        base = 0
        for q in range(k + 1, bit_count):
            base = base + (own[q] << (row_bits - 1 - (q - k - 1)))
        column = own[k] * row_count + base
        for group in range(1 << (bit_count - k - 1)):
            node = (
                subband_count
                - (subband_count >> level)
                + ((index >> (low_bit + bit_count)) << (bit_count - k - 1))
                + group
            )
            for row in range(2 * sources):
                low = 2 * group * sources + row // 2
                high = low + sources
                at = HALO + (group * 2 * sources + row) * block_count
                target[at : at + block_count, :] = source[
                    HALO + low * block_count : HALO + (low + 1) * block_count, :
                ] + delayed(source, HALO + high * block_count, shifts_ref[node, column + row], block_count)
        source, target = target, source
    return source


def gather_messages(sizes, low_bit, bit_count, msg_refs, first, second, shifts_ref):
    subband_count, row_count, block_count = sizes
    index = lax.axis_index("freq")
    power = jnp.zeros((HALO, LANES), jnp.float32)
    if len(msg_refs) > 1:
        core, chip = index & 1, (index >> 1) & 7
        count = 1 + len(MERGED_MASKS)
        merged, raw = msg_refs[:count], msg_refs[count:]
        for number, mask in enumerate(RAW_MASKS):
            for flip in range(2):
                ref = raw[2 * number + flip]
                at = HALO + (2 * number + (core ^ flip)) * block_count
                second[lines_at(at, block_count), :] = ref[HALO:, :]
                power = power + ref[:HALO, :]
        for number, mask in enumerate(RAW_MASKS):
            low = HALO + 2 * number * block_count
            for part in range(2):
                delay = shifts_ref[(index >> 1) ^ mask, core * row_count + 2 * reversed_bits(chip, 3) + part]
                at = HALO + (2 * (chip ^ mask) + part) * block_count
                first[lines_at(at, block_count), :] = second[low : low + block_count, :] + delayed(
                    second, low + block_count, delay, block_count
                )
        for mask, ref in zip((0,) + MERGED_MASKS, merged):
            at = HALO + 2 * (chip ^ mask) * block_count
            first[lines_at(at, 2 * block_count), :] = ref[HALO:, :]
            power = power + ref[:HALO, :]
        low_bit, bit_count = low_bit + 1, bit_count - 1
    else:
        (msg_ref,) = msg_refs
        span = (row_count >> bit_count) * block_count
        for message in range(1 << bit_count):
            at = HALO + reversed_bits(message, bit_count) * span
            start = message * (HALO + span)
            power = power + msg_ref[start : start + HALO, :]
            first[at : at + span, :] = msg_ref[start + HALO : start + HALO + span, :]
    final = tree_levels(first, second, shifts_ref, index, low_bit, bit_count, *sizes)
    return final, power


def merge_kernel(sizes, low_bit, bit_count, next_bits, shifts_ref, *refs):
    msg_refs, (out_ref, first, second) = refs[:-3], refs[-3:]
    _, row_count, block_count = sizes
    final, power = gather_messages(sizes, low_bit, bit_count, msg_refs, first, second, shifts_ref)
    span = (row_count >> next_bits) * block_count
    for message in range(1 << next_bits):
        start = message * (HALO + span)
        out_ref[start : start + HALO, :] = power
        out_ref[start + HALO : start + HALO + span, :] = final[HALO + message * span : HALO + (message + 1) * span, :]


def final_kernel(sizes, low_bit, bit_count, shifts_ref, prof_ref, *refs):
    msg_refs, (out_ref, first, second, windows, table) = refs[:-5], refs[-5:]
    subband_count, row_count, block_count = sizes
    prof_count, tap_count = prof_ref.shape
    span_len = table.shape[1]
    profiles = jnp.concatenate(
        [prof_ref[...].astype(jnp.float32), jnp.zeros((prof_count, span_len - tap_count), jnp.float32)], axis=1
    )
    for offset in range(HOLD):
        moved = profiles if offset == 0 else pltpu.roll(profiles, offset * STRIDE, 1)
        table[offset * prof_count : (offset + 1) * prof_count, :] = moved.astype(jnp.bfloat16)
    final, power = gather_messages(sizes, low_bit, bit_count, msg_refs, first, second, shifts_ref)
    line = lax.broadcasted_iota(jnp.int32, (block_count, LANES), 0)
    for row in range(row_count):
        for block in range(span_len // LANES):
            at = HALO + row * block_count + block
            piece = final[at : at + block_count, :]
            if block:
                piece = jnp.where(line < block_count - block, piece, 0.0)
            windows[row * block_count : (row + 1) * block_count, block * LANES : (block + 1) * LANES] = piece.astype(
                jnp.bfloat16
            )
    total = jnp.sum(jnp.sum(power, axis=0, keepdims=True), axis=1, keepdims=True)
    samples = subband_count * row_count * block_count * LANES
    rms_level = jnp.sqrt(subband_count * total / samples + 1e-06)
    group = 256 // block_count
    for start in range(0, row_count, group):
        products = lax.dot_general(
            table[...],
            windows[start * block_count : (start + group) * block_count, :],
            (((1,), (1,)), ((), ())),
            preferred_element_type=jnp.float32,
        )
        best = products[:prof_count]
        for offset in range(1, HOLD):
            best = jnp.maximum(best, products[offset * prof_count : (offset + 1) * prof_count])
        best = best / rms_level
        for row in range(group):
            out_ref[start + row] = best[:, row * block_count : (row + 1) * block_count].astype(jnp.bfloat16)


def stage_groups(subband_count, low_bit, bit_count):
    groups = []
    for rest in range(subband_count >> bit_count):
        low = rest & ((1 << low_bit) - 1)
        high = rest >> low_bit
        groups.append(
            [
                low + (reversed_bits(slot, bit_count) << low_bit) + (high << (low_bit + bit_count))
                for slot in range(1 << bit_count)
            ]
        )
    return groups


def exchange(value, mask):
    return lax.ppermute(value, "freq", [(source, source ^ mask) for source in range(lax.axis_size("freq"))])


def call(kernel, out_shape, in_specs, args, scratch=()):
    vmem = pl.BlockSpec(memory_space=pltpu.VMEM)
    return pl.pallas_call(
        kernel,
        out_shape=out_shape,
        in_specs=in_specs,
        out_specs=jax.tree.map(lambda _: vmem, out_shape),
        scratch_shapes=list(scratch),
        compiler_params=pltpu.CompilerParams(vmem_limit_bytes=VMEM_LIMIT),
    )(*args)


def per_device(spectra, profiles, shifts):
    row_count, time_len = spectra.shape
    prof_count, tap_count = profiles.shape
    subband_count = lax.axis_size("freq")
    level_count = subband_count.bit_length() - 1
    row_bits = row_count.bit_length() - 1
    block_count = time_len // LANES
    sizes = (subband_count, row_count, block_count)
    stages = []
    while sum(stages) < level_count:
        stages.append(min(row_bits, level_count - sum(stages)))
    vmem = pl.BlockSpec(memory_space=pltpu.VMEM)
    smem = pl.BlockSpec(memory_space=pltpu.SMEM)
    states = [pltpu.VMEM((row_count * block_count + 2 * HALO, LANES), jnp.float32)] * 2

    def lines(rows, tiles=1):
        return jax.ShapeDtypeStruct((rows * block_count + tiles * HALO, LANES), jnp.float32)

    def all_to_all(messages, low_bit, bit_count):
        shape = messages.shape
        pieces = messages.reshape(1 << bit_count, -1, LANES)
        groups = stage_groups(subband_count, low_bit, bit_count)
        return lax.all_to_all(pieces, "freq", 0, 0, tiled=True, axis_index_groups=groups).reshape(shape)

    if stages[0] == 4 and row_count == 16:
        half = row_count // 2
        *raw, sent, kept = call(
            split_kernel, [lines(1)] * (2 * len(RAW_MASKS)) + [lines(half)] * 2, [vmem], (spectra,)
        )
        got = exchange(sent, 1)
        raw = [exchange(value, 2 * mask + flip) for value, (mask, flip) in zip(raw, itertools.product(RAW_MASKS, (0, 1)))]
        own, *merged = call(
            functools.partial(core_merge_kernel, block_count, row_count),
            [lines(2)] * (1 + len(MERGED_MASKS)),
            [smem, vmem, vmem],
            (shifts, got, kept),
        )
        merged = [exchange(value, 2 * mask) for value, mask in zip(merged, MERGED_MASKS)]
        messages = [own, *merged, *raw]
    else:
        packed = call(pack_kernel, lines(row_count, 1 << stages[0]), [vmem], (spectra,))
        messages = [all_to_all(packed, 0, stages[0])]
    low_bit = 0
    for bit_count, next_bits in zip(stages[:-1], stages[1:]):
        packed = call(
            functools.partial(merge_kernel, sizes, low_bit, bit_count, next_bits),
            lines(row_count, 1 << next_bits),
            [smem] + [vmem] * len(messages),
            (shifts, *messages),
            states,
        )
        low_bit += bit_count
        messages = [all_to_all(packed, low_bit, next_bits)]
    block_len = STRIDE * HOLD
    extra = (tap_count + block_len - STRIDE - 1) // block_len
    span_len = (extra + 1) * block_len
    return call(
        functools.partial(final_kernel, sizes, low_bit, stages[-1]),
        jax.ShapeDtypeStruct((row_count, prof_count, block_count), jnp.bfloat16),
        [smem] + [vmem] * (1 + len(messages)),
        (shifts, profiles, *messages),
        states
        + [
            pltpu.VMEM((row_count * block_count, span_len), jnp.bfloat16),
            pltpu.VMEM((HOLD * prof_count, span_len), jnp.bfloat16),
        ],
    )


def solution(mesh):
    in_specs = (P(("beam", "freq"), None), P(), P())
    out_specs = P(("beam", "freq"), None, None)
    return jax.shard_map(
        per_device, mesh=mesh, in_specs=in_specs, out_specs=out_specs, check_vma=False
    )
```

```python
import functools

import jax
import jax.numpy as jnp
from jax import lax
from jax.experimental import pallas as pl
from jax.experimental.pallas import tpu as pltpu
from jax.sharding import PartitionSpec as P

STRIDE = 8
HOLD = 16
LANES = 128
HALO = 8
VMEM_LIMIT = 48 * 1024 * 1024
RAW_MASKS = (7, 6)
MERGED_MASKS = (5, 4, 3, 2, 1)
AFTER = 2


def reversed_bits(value, count):
    result = 0
    for bit in range(count):
        result |= ((value >> bit) & 1) << (count - 1 - bit)
    return result


def lines_at(start, count):
    return pl.ds(pl.multiple_of(start, 8), count)


def pack_rows(x_ref, store):
    row_count, time_len = x_ref.shape
    power = jnp.zeros((8, LANES), jnp.float32)
    for column in range(time_len // LANES):
        for half in range(row_count // 8):
            piece = x_ref[half * 8 : half * 8 + 8, column * LANES : (column + 1) * LANES]
            power = power + piece * piece
            store(half, column, piece)
    return power


def pack_kernel(x_ref, msg_ref):
    row_count, time_len = x_ref.shape
    block_count = time_len // LANES
    stride = HALO + block_count

    def store(half, column, piece):
        msg_ref[pl.ds(half * 8 * stride + HALO + column, 8, stride=stride), :] = piece

    power = pack_rows(x_ref, store)
    for row in range(row_count):
        msg_ref[row * stride : row * stride + HALO, :] = power


def split_kernel(x_ref, *refs):
    raw_refs, (sent_ref, kept_ref) = refs[:-2], refs[-2:]
    index = lax.axis_index("freq")
    core, chip = index & 1, (index >> 1) & 7
    row_count, time_len = x_ref.shape
    block_count = time_len // LANES
    half_span = row_count // 2 * block_count

    def body(own_half):
        def store(half, column, piece):
            ref = kept_ref if half == own_half else sent_ref
            ref[pl.ds(HALO + column, 8, stride=block_count), :] = piece

        power = pack_rows(x_ref, store)
        kept_ref[:HALO, :] = power
        sent_ref[:HALO, :] = power
        for number, mask in enumerate(RAW_MASKS):
            at = HALO + reversed_bits(chip ^ mask, 3) * block_count
            out_ref = raw_refs[number]
            out_ref[:HALO, :] = power
            out_ref[HALO : HALO + block_count, :] = sent_ref[lines_at(at, block_count), :]
            out_ref[HALO + block_count :, :] = kept_ref[lines_at(at, block_count), :]

    for own_half in range(2):
        pl.when(core == own_half)(functools.partial(body, own_half))


def delayed(source, high, delay, block_count):
    lane = lax.broadcasted_iota(jnp.int32, (block_count, LANES), 1)
    line = lax.broadcasted_iota(jnp.int32, (HALO, LANES), 0)
    lines, part = delay >> 7, delay & (LANES - 1)
    near = source[pl.ds(high - lines, block_count), :]
    far = source[pl.ds(high - lines - 1, block_count), :]
    moved = pltpu.roll(jnp.where(lane < LANES - part, near, far), part, 1)
    head = jnp.where(line * LANES + lane[:HALO] >= delay, moved[:HALO], 0.0)
    return jnp.concatenate([head, moved[HALO:]], axis=0)


def core_merge_kernel(block_count, row_count, shifts_ref, got_ref, kept_ref, *outs):
    index = lax.axis_index("freq")
    core, chip = index & 1, (index >> 1) & 7

    def body(low_ref, high_ref):
        power = low_ref[:HALO, :] + high_ref[:HALO, :]
        for mask, out_ref in zip((0,) + MERGED_MASKS, outs):
            place = reversed_bits(chip ^ mask, 3)
            at = HALO + place * block_count
            for part in range(2):
                delay = shifts_ref[index >> 1, core * row_count + 2 * place + part]
                out_ref[HALO + part * block_count : HALO + (part + 1) * block_count, :] = low_ref[
                    lines_at(at, block_count), :
                ] + delayed(high_ref, at, delay, block_count)
            out_ref[:HALO, :] = power

    pl.when(core == 0)(lambda: body(kept_ref, got_ref))
    pl.when(core == 1)(lambda: body(got_ref, kept_ref))


def pass_kernel(block_count, *refs):
    raw_refs, out_ref = refs[: len(RAW_MASKS)], refs[-1]
    power = raw_refs[0][:HALO, :]
    for ref in raw_refs[1:]:
        power = power + ref[:HALO, :]
    out_ref[:HALO, :] = power
    for number, ref in enumerate(raw_refs):
        out_ref[HALO + number * block_count : HALO + (number + 1) * block_count, :] = ref[HALO : HALO + block_count, :]


def tree_levels(first, second, shifts_ref, index, low_bit, bit_count, subband_count, row_count, block_count):
    row_bits = row_count.bit_length() - 1
    own = [(index >> (low_bit + k)) & 1 for k in range(bit_count)]
    source, target = first, second
    for k in range(bit_count):
        level = low_bit + k
        sources = 1 << (row_bits - bit_count + k)
        base = 0
        for q in range(k + 1, bit_count):
            base = base + (own[q] << (row_bits - 1 - (q - k - 1)))
        column = own[k] * row_count + base
        for group in range(1 << (bit_count - k - 1)):
            node = (
                subband_count
                - (subband_count >> level)
                + ((index >> (low_bit + bit_count)) << (bit_count - k - 1))
                + group
            )
            for row in range(2 * sources):
                low = 2 * group * sources + row // 2
                high = low + sources
                at = HALO + (group * 2 * sources + row) * block_count
                target[at : at + block_count, :] = source[
                    HALO + low * block_count : HALO + (low + 1) * block_count, :
                ] + delayed(source, HALO + high * block_count, shifts_ref[node, column + row], block_count)
        source, target = target, source
    return source


def gather_messages(sizes, low_bit, bit_count, msg_refs, first, second, shifts_ref):
    subband_count, row_count, block_count = sizes
    index = lax.axis_index("freq")
    power = jnp.zeros((HALO, LANES), jnp.float32)
    if len(msg_refs) > 1:
        core, chip = index & 1, (index >> 1) & 7
        count = 1 + len(MERGED_MASKS)
        merged, raw, passed_refs = msg_refs[:count], msg_refs[count : count + len(RAW_MASKS)], msg_refs[count + len(RAW_MASKS) :]
        for number, mask in enumerate(RAW_MASKS):
            ref = raw[number]
            at = HALO + (2 * number + core) * block_count
            second[lines_at(at, block_count), :] = ref[HALO + block_count :, :]
            at = HALO + (2 * number + 1 - core) * block_count
            second[lines_at(at, block_count), :] = passed_refs[0][
                HALO + number * block_count : HALO + (number + 1) * block_count, :
            ]
            power = power + ref[:HALO, :]
        if RAW_MASKS:
            power = power + passed_refs[0][:HALO, :]
        for number, mask in enumerate(RAW_MASKS):
            low = HALO + 2 * number * block_count
            for part in range(2):
                delay = shifts_ref[(index >> 1) ^ mask, core * row_count + 2 * reversed_bits(chip, 3) + part]
                at = HALO + (2 * (chip ^ mask) + part) * block_count
                first[lines_at(at, block_count), :] = second[low : low + block_count, :] + delayed(
                    second, low + block_count, delay, block_count
                )
        for mask, ref in zip((0,) + MERGED_MASKS, merged):
            at = HALO + 2 * (chip ^ mask) * block_count
            first[lines_at(at, 2 * block_count), :] = ref[HALO:, :]
            power = power + ref[:HALO, :]
        low_bit, bit_count = low_bit + 1, bit_count - 1
    else:
        (msg_ref,) = msg_refs
        span = (row_count >> bit_count) * block_count
        for message in range(1 << bit_count):
            at = HALO + reversed_bits(message, bit_count) * span
            start = message * (HALO + span)
            power = power + msg_ref[start : start + HALO, :]
            first[at : at + span, :] = msg_ref[start + HALO : start + HALO + span, :]
    final = tree_levels(first, second, shifts_ref, index, low_bit, bit_count, *sizes)
    return final, power


def merge_kernel(sizes, low_bit, bit_count, next_bits, shifts_ref, *refs):
    msg_refs, (out_ref, first, second) = refs[:-3], refs[-3:]
    _, row_count, block_count = sizes
    final, power = gather_messages(sizes, low_bit, bit_count, msg_refs, first, second, shifts_ref)
    span = (row_count >> next_bits) * block_count
    for message in range(1 << next_bits):
        start = message * (HALO + span)
        out_ref[start : start + HALO, :] = power
        out_ref[start + HALO : start + HALO + span, :] = final[HALO + message * span : HALO + (message + 1) * span, :]


def final_kernel(sizes, low_bit, bit_count, shifts_ref, prof_ref, *refs):
    msg_refs, (out_ref, first, second, windows, table) = refs[:-5], refs[-5:]
    subband_count, row_count, block_count = sizes
    prof_count, tap_count = prof_ref.shape
    span_len = table.shape[1]
    profiles = jnp.concatenate(
        [prof_ref[...].astype(jnp.float32), jnp.zeros((prof_count, span_len - tap_count), jnp.float32)], axis=1
    )
    for offset in range(HOLD):
        moved = profiles if offset == 0 else pltpu.roll(profiles, offset * STRIDE, 1)
        table[offset * prof_count : (offset + 1) * prof_count, :] = moved.astype(jnp.bfloat16)
    final, power = gather_messages(sizes, low_bit, bit_count, msg_refs, first, second, shifts_ref)
    line = lax.broadcasted_iota(jnp.int32, (block_count, LANES), 0)
    for row in range(row_count):
        for block in range(span_len // LANES):
            at = HALO + row * block_count + block
            piece = final[at : at + block_count, :]
            if block:
                piece = jnp.where(line < block_count - block, piece, 0.0)
            windows[row * block_count : (row + 1) * block_count, block * LANES : (block + 1) * LANES] = piece.astype(
                jnp.bfloat16
            )
    total = jnp.sum(jnp.sum(power, axis=0, keepdims=True), axis=1, keepdims=True)
    samples = subband_count * row_count * block_count * LANES
    rms_level = jnp.sqrt(subband_count * total / samples + 1e-06)
    group = 256 // block_count
    for start in range(0, row_count, group):
        products = lax.dot_general(
            table[...],
            windows[start * block_count : (start + group) * block_count, :],
            (((1,), (1,)), ((), ())),
            preferred_element_type=jnp.float32,
        )
        best = products[:prof_count]
        for offset in range(1, HOLD):
            best = jnp.maximum(best, products[offset * prof_count : (offset + 1) * prof_count])
        best = best / rms_level
        for row in range(group):
            out_ref[start + row] = best[:, row * block_count : (row + 1) * block_count].astype(jnp.bfloat16)


def stage_groups(subband_count, low_bit, bit_count):
    groups = []
    for rest in range(subband_count >> bit_count):
        low = rest & ((1 << low_bit) - 1)
        high = rest >> low_bit
        groups.append(
            [
                low + (reversed_bits(slot, bit_count) << low_bit) + (high << (low_bit + bit_count))
                for slot in range(1 << bit_count)
            ]
        )
    return groups


def exchange(value, mask):
    return lax.ppermute(value, "freq", [(source, source ^ mask) for source in range(lax.axis_size("freq"))])


def call(kernel, out_shape, in_specs, args, scratch=()):
    vmem = pl.BlockSpec(memory_space=pltpu.VMEM)
    return pl.pallas_call(
        kernel,
        out_shape=out_shape,
        in_specs=in_specs,
        out_specs=jax.tree.map(lambda _: vmem, out_shape),
        scratch_shapes=list(scratch),
        compiler_params=pltpu.CompilerParams(vmem_limit_bytes=VMEM_LIMIT),
    )(*args)


def per_device(spectra, profiles, shifts):
    row_count, time_len = spectra.shape
    prof_count, tap_count = profiles.shape
    subband_count = lax.axis_size("freq")
    level_count = subband_count.bit_length() - 1
    row_bits = row_count.bit_length() - 1
    block_count = time_len // LANES
    sizes = (subband_count, row_count, block_count)
    stages = []
    while sum(stages) < level_count:
        stages.append(min(row_bits, level_count - sum(stages)))
    vmem = pl.BlockSpec(memory_space=pltpu.VMEM)
    smem = pl.BlockSpec(memory_space=pltpu.SMEM)
    states = [pltpu.VMEM((row_count * block_count + 2 * HALO, LANES), jnp.float32)] * 2

    def lines(rows, tiles=1):
        return jax.ShapeDtypeStruct((rows * block_count + tiles * HALO, LANES), jnp.float32)

    def all_to_all(messages, low_bit, bit_count):
        shape = messages.shape
        pieces = messages.reshape(1 << bit_count, -1, LANES)
        groups = stage_groups(subband_count, low_bit, bit_count)
        return lax.all_to_all(pieces, "freq", 0, 0, tiled=True, axis_index_groups=groups).reshape(shape)

    if stages[0] == 4 and row_count == 16:
        half = row_count // 2
        *raw, sent, kept = call(
            split_kernel, [lines(2)] * len(RAW_MASKS) + [lines(half)] * 2, [vmem], (spectra,)
        )
        raw = [exchange(value, 2 * mask) for value, mask in zip(raw, RAW_MASKS)]
        got = exchange(sent, 1)
        own, *merged = call(
            functools.partial(core_merge_kernel, block_count, row_count),
            [lines(2)] * (1 + len(MERGED_MASKS)),
            [smem, vmem, vmem],
            (shifts, got, kept),
        )
        merged = [exchange(value, 2 * mask) for value, mask in zip(merged, MERGED_MASKS)]
        messages = [own, *merged, *raw]
        if RAW_MASKS:
            passed = call(
                functools.partial(pass_kernel, block_count),
                lines(len(RAW_MASKS)),
                [vmem] * (1 + len(RAW_MASKS)),
                (*raw, merged[AFTER]),
            )
            messages.append(exchange(passed, 1))
    else:
        packed = call(pack_kernel, lines(row_count, 1 << stages[0]), [vmem], (spectra,))
        messages = [all_to_all(packed, 0, stages[0])]
    low_bit = 0
    for bit_count, next_bits in zip(stages[:-1], stages[1:]):
        packed = call(
            functools.partial(merge_kernel, sizes, low_bit, bit_count, next_bits),
            lines(row_count, 1 << next_bits),
            [smem] + [vmem] * len(messages),
            (shifts, *messages),
            states,
        )
        low_bit += bit_count
        messages = [all_to_all(packed, low_bit, next_bits)]
    block_len = STRIDE * HOLD
    extra = (tap_count + block_len - STRIDE - 1) // block_len
    span_len = (extra + 1) * block_len
    return call(
        functools.partial(final_kernel, sizes, low_bit, stages[-1]),
        jax.ShapeDtypeStruct((row_count, prof_count, block_count), jnp.bfloat16),
        [smem] + [vmem] * (1 + len(messages)),
        (shifts, profiles, *messages),
        states
        + [
            pltpu.VMEM((row_count * block_count, span_len), jnp.bfloat16),
            pltpu.VMEM((HOLD * prof_count, span_len), jnp.bfloat16),
        ],
    )


def solution(mesh):
    in_specs = (P(("beam", "freq"), None), P(), P())
    out_specs = P(("beam", "freq"), None, None)
    return jax.shard_map(
        per_device, mesh=mesh, in_specs=in_specs, out_specs=out_specs, check_vma=False
    )
```

```python
import functools

import jax
import jax.numpy as jnp
from jax import lax
from jax.experimental import pallas as pl
from jax.experimental.pallas import tpu as pltpu
from jax.sharding import PartitionSpec as P

STRIDE = 8
HOLD = 16
LANES = 128
HALO = 8
VMEM_LIMIT = 48 * 1024 * 1024
FETCHES = 4
RAW_MASKS = (7, 5)
MERGED_MASKS = (4, 6, 3, 2, 1)
PASS_AFTER = 3


def reversed_bits(value, count):
    result = 0
    for bit in range(count):
        result |= ((value >> bit) & 1) << (count - 1 - bit)
    return result


def lines_at(start, count):
    return pl.ds(pl.multiple_of(start, 8), count)


def aligned_rows(x_ref, buffer, sems, store):
    row_count, time_len = x_ref.shape
    width = time_len // FETCHES
    copies = []
    for part in range(FETCHES):
        for half in range(row_count // 8):
            at = (pl.ds(half * 8, 8), pl.ds(part * width, width))
            copies.append(pltpu.make_async_copy(x_ref.at[at], buffer.at[at], sems.at[len(copies)]))
    for copy in copies:
        copy.start()
    power = jnp.zeros((8, LANES), jnp.float32)
    for part in range(FETCHES):
        for half in range(row_count // 8):
            copies[part * (row_count // 8) + half].wait()
            for column in range(part * width // LANES, (part + 1) * width // LANES):
                piece = buffer[half * 8 : half * 8 + 8, column * LANES : (column + 1) * LANES]
                power = power + piece * piece
                store(half, column, piece)
    return power


def pack_kernel(x_ref, msg_ref, buffer, sems):
    row_count, time_len = x_ref.shape
    block_count = time_len // LANES
    stride = HALO + block_count

    def store(half, column, piece):
        msg_ref[pl.ds(half * 8 * stride + HALO + column, 8, stride=stride), :] = piece

    power = aligned_rows(x_ref, buffer, sems, store)
    for row in range(row_count):
        msg_ref[row * stride : row * stride + HALO, :] = power


def split_kernel(x_ref, *refs):
    raw_refs, (sent_ref, kept_ref, rows, buffer, sems) = refs[:-5], refs[-5:]
    index = lax.axis_index("freq")
    core, chip = index & 1, (index >> 1) & 7
    row_count, time_len = x_ref.shape
    block_count = time_len // LANES
    half_rows = row_count // 2
    stride = block_count + HALO

    def store(half, column, piece):
        rows[pl.ds(half * 8 * stride + column, 8, stride=stride), :] = piece

    power = aligned_rows(x_ref, buffer, sems, store)
    for ref in (*raw_refs, sent_ref, kept_ref):
        ref[:HALO, :] = power
    sent_at, kept_at = (1 - core) * half_rows * stride, core * half_rows * stride
    for mask, out_ref in zip(RAW_MASKS, raw_refs):
        at = reversed_bits(chip ^ mask, 3) * stride
        out_ref[HALO : HALO + block_count, :] = rows[lines_at(sent_at + at, block_count), :]
        out_ref[HALO + block_count :, :] = rows[lines_at(kept_at + at, block_count), :]
    for row in range(half_rows):
        for ref, at in ((sent_ref, sent_at), (kept_ref, kept_at)):
            ref[HALO + row * block_count : HALO + (row + 1) * block_count, :] = rows[
                lines_at(at + row * stride, block_count), :
            ]


def delays_at(shifts_ref, node, groups, column, count):
    rows = shifts_ref[pl.ds(node, groups), :]
    rows = jnp.concatenate([rows, jnp.zeros((groups, LANES - rows.shape[1]), jnp.int32)], axis=1)
    rows = pltpu.roll(rows, (LANES - column) & (LANES - 1), 1)
    return [[rows[group, row] for row in range(count)] for group in range(groups)]


def delayed(source, high, delay, block_count):
    lane = lax.broadcasted_iota(jnp.int32, (block_count, LANES), 1)
    line = lax.broadcasted_iota(jnp.int32, (HALO, LANES), 0)
    lines, part = delay >> 7, delay & (LANES - 1)
    near = source[pl.ds(high - lines, block_count), :]
    far = source[pl.ds(high - lines - 1, block_count), :]
    moved = pltpu.roll(jnp.where(lane < LANES - part, near, far), part, 1)
    head = jnp.where(line * LANES + lane[:HALO] >= delay, moved[:HALO], 0.0)
    return jnp.concatenate([head, moved[HALO:]], axis=0)


def merge(source, low, high, delays, target, at, block_count, rows=None):
    for row in range(len(delays)) if rows is None else rows:
        skip = row // 2 * block_count
        target[lines_at(at + row * block_count, block_count), :] = source[
            lines_at(low + skip, block_count), :
        ] + delayed(source, high + skip, delays[row], block_count)


def core_merge_kernel(block_count, row_count, shifts_ref, got_ref, kept_ref, *outs):
    index = lax.axis_index("freq")
    core, chip = index & 1, (index >> 1) & 7
    row = jnp.broadcast_to(shifts_ref[pl.ds(index >> 1, 1), :], (row_count, 2 * row_count))
    entry = lax.broadcasted_iota(jnp.int32, row.shape, 0) ^ (2 * reversed_bits(chip, 3))
    column = lax.broadcasted_iota(jnp.int32, row.shape, 1)
    picked = jnp.where(column == entry + core * row_count, row.astype(jnp.float32), 0.0)
    picked = jnp.sum(picked, axis=1, keepdims=True).astype(jnp.int32)

    def body(low_ref, high_ref):
        power = low_ref[:HALO, :] + high_ref[:HALO, :]
        for mask, out_ref in zip((0,) + MERGED_MASKS, outs):
            at = HALO + reversed_bits(chip ^ mask, 3) * block_count
            for part in range(2):
                delay = picked[2 * reversed_bits(mask, 3) + part, 0]
                out_ref[HALO + part * block_count : HALO + (part + 1) * block_count, :] = low_ref[
                    lines_at(at, block_count), :
                ] + delayed(high_ref, at, delay, block_count)
            out_ref[:HALO, :] = power

    pl.when(core == 0)(lambda: body(kept_ref, got_ref))
    pl.when(core == 1)(lambda: body(got_ref, kept_ref))


def pass_kernel(block_count, *refs):
    raw_refs, out_ref = refs[: len(RAW_MASKS)], refs[-1]
    power = raw_refs[0][:HALO, :]
    for ref in raw_refs[1:]:
        power = power + ref[:HALO, :]
    out_ref[:HALO, :] = power
    for number, ref in enumerate(raw_refs):
        out_ref[HALO + number * block_count : HALO + (number + 1) * block_count, :] = ref[HALO : HALO + block_count, :]


class Chip:
    def __init__(self, sizes, shifts_ref):
        self.subband_count, self.row_count, self.block_count = sizes
        self.shifts_ref = shifts_ref
        self.index = lax.axis_index("freq")
        self.core, self.chip, self.upper = self.index & 1, (self.index >> 1) & 7, self.index >> 4
        self.y, self.z, self.far = self.chip & 1, (self.chip >> 1) & 1, (self.chip >> 2) & 1

    def delays(self, level, group):
        bits = (self.core, self.y, self.z, self.far)
        node = self.subband_count - (self.subband_count >> level) + (self.upper << (3 - level)) + group
        column = bits[level] * self.row_count
        for above in range(level + 1, 4):
            column = column + (bits[above] << (4 + level - above))
        return delays_at(self.shifts_ref, node, 1, column, 2 << level)[0]


def chip_levels(sizes, shifts_ref, *refs):
    count = 1 + len(MERGED_MASKS)
    merged, raw, (passed_ref, first, second) = refs[:count], refs[count:-3], refs[-3:]
    here = Chip(sizes, shifts_ref)
    block_count = here.block_count
    power = passed_ref[:HALO, :]
    for number, (mask, ref) in enumerate(zip(RAW_MASKS, raw)):
        base = HALO + 2 * number * block_count
        own, other = here.core * block_count, (1 - here.core) * block_count
        second[lines_at(base + own, block_count), :] = ref[HALO + block_count :, :]
        at = HALO + number * block_count
        second[lines_at(base + other, block_count), :] = passed_ref[at : at + block_count, :]
        delays = here.delays(0, here.chip ^ mask)
        at = HALO + (here.chip ^ mask) * 2 * block_count
        merge(second, base, base + block_count, delays, first, at, block_count)
        power = power + ref[:HALO, :]
    for mask, ref in zip((0,) + MERGED_MASKS, merged):
        first[lines_at(HALO + (here.chip ^ mask) * 2 * block_count, 2 * block_count), :] = ref[HALO:, :]
        power = power + ref[:HALO, :]
    for level in range(1, 3):
        span = block_count << level
        for group in range(8 >> level):
            at = HALO + 2 * span * group
            merge(first, at, at + span, here.delays(level, group), second, at, block_count)
        first, second = second, first
    last = functools.partial(merge, first, HALO, HALO + 8 * block_count, here.delays(3, 0), second, HALO, block_count)
    return last, second, power


def packed_levels(sizes, low_bit, bit_count, shifts_ref, msg_ref, first, second):
    subband_count, row_count, block_count = sizes
    row_bits = row_count.bit_length() - 1
    index = lax.axis_index("freq")
    power = jnp.zeros((HALO, LANES), jnp.float32)
    span = (row_count >> bit_count) * block_count
    for message in range(1 << bit_count):
        at = HALO + reversed_bits(message, bit_count) * span
        start = message * (HALO + span)
        power = power + msg_ref[start : start + HALO, :]
        first[at : at + span, :] = msg_ref[start + HALO : start + HALO + span, :]
    own = [(index >> (low_bit + k)) & 1 for k in range(bit_count)]
    source, target = first, second
    for k in range(bit_count):
        level = low_bit + k
        span = (1 << (row_bits - bit_count + k)) * block_count
        column = own[k] * row_count
        for q in range(k + 1, bit_count):
            column = column + (own[q] << (row_bits - q + k))
        groups = 1 << (bit_count - k - 1)
        node = subband_count - (subband_count >> level) + ((index >> (low_bit + bit_count)) << (bit_count - k - 1))
        delays = delays_at(shifts_ref, node, groups, column, 2 * span // block_count)
        for group in range(groups):
            at = HALO + 2 * group * span
            last = functools.partial(merge, source, at, at + span, delays[group], target, at, block_count)
            if groups > 1:
                last()
        source, target = target, source
    return last, source, power


def merge_kernel(sizes, levels, next_bits, shifts_ref, *refs):
    msg_refs, (out_ref, first, second) = refs[:-3], refs[-3:]
    _, row_count, block_count = sizes
    last, final, power = levels(shifts_ref, *msg_refs, first, second)
    last()
    span = (row_count >> next_bits) * block_count
    for message in range(1 << next_bits):
        start = message * (HALO + span)
        out_ref[start : start + HALO, :] = power
        out_ref[start + HALO : start + HALO + span, :] = final[HALO + message * span : HALO + (message + 1) * span, :]


def table_kernel(prof_ref, after_ref, table_ref):
    prof_count, tap_count = prof_ref.shape
    span_len = table_ref.shape[1]
    profiles = jnp.concatenate(
        [prof_ref[...].astype(jnp.float32), jnp.zeros((prof_count, span_len - tap_count), jnp.float32)], axis=1
    )
    for offset in range(HOLD):
        moved = profiles if offset == 0 else pltpu.roll(profiles, offset * STRIDE, 1)
        table_ref[offset * prof_count : (offset + 1) * prof_count, :] = moved.astype(jnp.bfloat16)


def final_kernel(sizes, levels, shifts_ref, table_ref, *refs):
    msg_refs, (out_ref, first, second, windows) = refs[:-4], refs[-4:]
    subband_count, row_count, block_count = sizes
    prof_count = table_ref.shape[0] // HOLD
    last, final, power = levels(shifts_ref, *msg_refs, first, second)
    total = jnp.sum(jnp.sum(power, axis=0, keepdims=True), axis=1, keepdims=True)
    samples = subband_count * row_count * block_count * LANES
    rms_level = jnp.sqrt(subband_count * total / samples + 1e-06)
    line = lax.broadcasted_iota(jnp.int32, (block_count, LANES), 0)
    group = 256 // block_count
    for start in range(0, row_count, group):
        last(rows=range(start, start + group))
        for row in range(start, start + group):
            for block in range(table_ref.shape[1] // LANES):
                at = HALO + row * block_count + block
                piece = final[at : at + block_count, :]
                if block:
                    piece = jnp.where(line < block_count - block, piece, 0.0)
                windows[
                    row * block_count : (row + 1) * block_count, block * LANES : (block + 1) * LANES
                ] = piece.astype(jnp.bfloat16)
        products = lax.dot_general(
            table_ref[...],
            windows[start * block_count : (start + group) * block_count, :],
            (((1,), (1,)), ((), ())),
            preferred_element_type=jnp.float32,
        )
        best = products[:prof_count]
        for offset in range(1, HOLD):
            best = jnp.maximum(best, products[offset * prof_count : (offset + 1) * prof_count])
        best = best / rms_level
        for row in range(group):
            out_ref[start + row] = best[:, row * block_count : (row + 1) * block_count].astype(jnp.bfloat16)


def stage_groups(subband_count, low_bit, bit_count):
    groups = []
    for rest in range(subband_count >> bit_count):
        low = rest & ((1 << low_bit) - 1)
        high = rest >> low_bit
        groups.append(
            [
                low + (reversed_bits(slot, bit_count) << low_bit) + (high << (low_bit + bit_count))
                for slot in range(1 << bit_count)
            ]
        )
    return groups


def exchange(value, mask):
    return lax.ppermute(value, "freq", [(source, source ^ mask) for source in range(lax.axis_size("freq"))])


def call(kernel, out_shape, args, scratch=(), space=pltpu.VMEM):
    vmem = pl.BlockSpec(memory_space=pltpu.VMEM)
    return pl.pallas_call(
        kernel,
        out_shape=out_shape,
        in_specs=[pl.BlockSpec(memory_space=space)] * len(args),
        out_specs=jax.tree.map(lambda _: vmem, out_shape),
        scratch_shapes=list(scratch),
        compiler_params=pltpu.CompilerParams(vmem_limit_bytes=VMEM_LIMIT),
    )(*args)


def per_device(spectra, profiles, shifts):
    row_count, time_len = spectra.shape
    prof_count, tap_count = profiles.shape
    subband_count = lax.axis_size("freq")
    level_count = subband_count.bit_length() - 1
    row_bits = row_count.bit_length() - 1
    block_count = time_len // LANES
    sizes = (subband_count, row_count, block_count)
    stages = []
    while sum(stages) < level_count:
        stages.append(min(row_bits, level_count - sum(stages)))
    spectra = pltpu.with_memory_space_constraint(spectra, pltpu.HBM)
    states = [pltpu.VMEM((row_count * block_count + 2 * HALO, LANES), jnp.float32)] * 2
    fetch = [
        pltpu.VMEM(spectra.shape, jnp.float32),
        pltpu.SemaphoreType.DMA((FETCHES * row_count // 8,)),
    ]

    def lines(rows, tiles=1):
        return jax.ShapeDtypeStruct((rows * block_count + tiles * HALO, LANES), jnp.float32)

    def all_to_all(messages, low_bit, bit_count):
        shape = messages.shape
        pieces = messages.reshape(1 << bit_count, -1, LANES)
        groups = stage_groups(subband_count, low_bit, bit_count)
        return lax.all_to_all(pieces, "freq", 0, 0, tiled=True, axis_index_groups=groups).reshape(shape)

    if stages[0] == 4 and row_count == 16:
        half = row_count // 2
        *raw, sent, kept = call(
            split_kernel,
            [lines(2)] * len(RAW_MASKS) + [lines(half)] * 2,
            (spectra,),
            [pltpu.VMEM((row_count * (block_count + HALO), LANES), jnp.float32)] + fetch,
            pltpu.HBM,
        )
        raw = {mask: exchange(value, 2 * mask) for mask, value in zip(RAW_MASKS, raw)}
        got = exchange(sent, 1)
        own, *merged = call(
            functools.partial(core_merge_kernel, block_count, row_count),
            [lines(2)] * (1 + len(MERGED_MASKS)),
            (shifts, got, kept),
        )
        merged = {mask: exchange(value, 2 * mask) for mask, value in zip(MERGED_MASKS, merged)}
        passed = call(
            functools.partial(pass_kernel, block_count),
            lines(len(RAW_MASKS)),
            (*raw.values(), merged[PASS_AFTER]),
        )
        passed = exchange(passed, 1)
        after = own
        messages = [own, *merged.values(), *raw.values(), passed]
        levels = functools.partial(chip_levels, sizes)
    else:
        packed = call(pack_kernel, lines(row_count, 1 << stages[0]), (spectra,), fetch, pltpu.HBM)
        after = packed
        messages = [all_to_all(packed, 0, stages[0])]
        levels = functools.partial(packed_levels, sizes, 0, stages[0])
    low_bit = 0
    for bit_count, next_bits in zip(stages[:-1], stages[1:]):
        packed = call(
            functools.partial(merge_kernel, sizes, levels, next_bits),
            lines(row_count, 1 << next_bits),
            (shifts, *messages),
            states,
        )
        low_bit += bit_count
        messages = [all_to_all(packed, low_bit, next_bits)]
        levels = functools.partial(packed_levels, sizes, low_bit, next_bits)
    block_len = STRIDE * HOLD
    extra = (tap_count + block_len - STRIDE - 1) // block_len
    span_len = (extra + 1) * block_len
    table = call(table_kernel, jax.ShapeDtypeStruct((HOLD * prof_count, span_len), jnp.bfloat16), (profiles, after))
    return call(
        functools.partial(final_kernel, sizes, levels),
        jax.ShapeDtypeStruct((row_count, prof_count, block_count), jnp.bfloat16),
        (shifts, table, *messages),
        states + [pltpu.VMEM((row_count * block_count, span_len), jnp.bfloat16)],
    )


def solution(mesh):
    in_specs = (P(("beam", "freq"), None), P(), P())
    out_specs = P(("beam", "freq"), None, None)
    return jax.shard_map(
        per_device, mesh=mesh, in_specs=in_specs, out_specs=out_specs, check_vma=False
    )
```

```python
import functools

import jax
import jax.numpy as jnp
from jax import lax
from jax.experimental import pallas as pl
from jax.experimental.pallas import tpu as pltpu
from jax.sharding import PartitionSpec as P

STRIDE = 8
HOLD = 16
LANES = 128
HALO = 8
GROUP = 256
VMEM_LIMIT = 48 * 1024 * 1024
FETCHES = 4
RAW_MASKS = (7, 5)
MERGED_MASKS = (4, 6, 3, 2, 1)
PASS_AFTER = 3


def reversed_bits(value, count):
    result = 0
    for bit in range(count):
        result |= ((value >> bit) & 1) << (count - 1 - bit)
    return result


def lines_at(start, count):
    if isinstance(start, int):
        return slice(start, start + count)
    return pl.ds(pl.multiple_of(start, 8), count)


def aligned_rows(x_ref, buffer, sems, store):
    row_count, time_len = x_ref.shape
    width = time_len // FETCHES
    copies = []
    for part in range(FETCHES):
        for half in range(row_count // 8):
            at = (pl.ds(half * 8, 8), pl.ds(part * width, width))
            copies.append(pltpu.make_async_copy(x_ref.at[at], buffer.at[at], sems.at[len(copies)]))
    for copy in copies:
        copy.start()
    power = jnp.zeros((8, LANES), jnp.float32)
    for part in range(FETCHES):
        for half in range(row_count // 8):
            copies[part * (row_count // 8) + half].wait()
            for column in range(part * width // LANES, (part + 1) * width // LANES):
                piece = buffer[half * 8 : half * 8 + 8, column * LANES : (column + 1) * LANES]
                power = power + piece * piece
                store(half, column, piece)
    return power


def pack_kernel(x_ref, msg_ref, buffer, sems):
    row_count, time_len = x_ref.shape
    block_count = time_len // LANES
    stride = HALO + block_count

    def store(half, column, piece):
        msg_ref[pl.ds(half * 8 * stride + HALO + column, 8, stride=stride), :] = piece

    power = aligned_rows(x_ref, buffer, sems, store)
    for row in range(row_count):
        msg_ref[row * stride : row * stride + HALO, :] = power


def split_kernel(x_ref, *refs):
    raw_refs, (sent_ref, kept_ref, buffer, sems) = refs[:-4], refs[-4:]
    index = lax.axis_index("freq")
    core, chip = index & 1, (index >> 1) & 7
    row_count, time_len = x_ref.shape
    block_count = time_len // LANES
    stride = block_count + HALO

    def body(own_half):
        def store(half, column, piece):
            ref = kept_ref if half == own_half else sent_ref
            ref[pl.ds(HALO + column, 8, stride=stride), :] = piece

        power = aligned_rows(x_ref, buffer, sems, store)
        for mask, out_ref in zip(RAW_MASKS, raw_refs):
            at = HALO + reversed_bits(chip ^ mask, 3) * stride
            out_ref[:HALO, :] = power
            out_ref[HALO : HALO + block_count, :] = sent_ref[lines_at(at, block_count), :]
            out_ref[HALO + block_count :, :] = kept_ref[lines_at(at, block_count), :]
        for ref in (sent_ref, kept_ref):
            ref[:HALO, :] = power

    for own_half in range(2):
        pl.when(core == own_half)(functools.partial(body, own_half))


def delays_at(shifts_ref, node, groups, column, count):
    rows = shifts_ref[pl.ds(node, groups), :]
    rows = jnp.concatenate([rows, jnp.zeros((groups, LANES - rows.shape[1]), jnp.int32)], axis=1)
    rows = pltpu.roll(rows, (LANES - column) & (LANES - 1), 1)
    return [[rows[group, row] for row in range(count)] for group in range(groups)]


def delayed(source, high, delay, block_count):
    lane = lax.broadcasted_iota(jnp.int32, (block_count, LANES), 1)
    line = lax.broadcasted_iota(jnp.int32, (HALO, LANES), 0)
    lines, part = delay >> 7, delay & (LANES - 1)
    near = source[pl.ds(high - lines, block_count), :]
    far = source[pl.ds(high - lines - 1, block_count), :]
    moved = pltpu.roll(jnp.where(lane < LANES - part, near, far), part, 1)
    head = jnp.where(line * LANES + lane[:HALO] >= delay, moved[:HALO], 0.0)
    return jnp.concatenate([head, moved[HALO:]], axis=0)


def merge(source, low, high, delays, target, at, block_count, rows=None):
    for row in range(len(delays)) if rows is None else rows:
        skip = row // 2 * block_count
        target[lines_at(at + row * block_count, block_count), :] = source[
            lines_at(low + skip, block_count), :
        ] + delayed(source, high + skip, delays[row], block_count)


def core_merge_kernel(block_count, row_count, shifts_ref, got_ref, kept_ref, *outs):
    index = lax.axis_index("freq")
    core, chip = index & 1, (index >> 1) & 7
    row = jnp.broadcast_to(shifts_ref[pl.ds(index >> 1, 1), :], (row_count, 2 * row_count))
    entry = lax.broadcasted_iota(jnp.int32, row.shape, 0) ^ (2 * reversed_bits(chip, 3))
    column = lax.broadcasted_iota(jnp.int32, row.shape, 1)
    picked = jnp.where(column == entry + core * row_count, row.astype(jnp.float32), 0.0)
    picked = jnp.sum(picked, axis=1, keepdims=True).astype(jnp.int32)

    def body(low_ref, high_ref):
        power = low_ref[:HALO, :] + high_ref[:HALO, :]
        for mask, out_ref in zip((0,) + MERGED_MASKS, outs):
            at = HALO + reversed_bits(chip ^ mask, 3) * (block_count + HALO)
            for part in range(2):
                delay = picked[2 * reversed_bits(mask, 3) + part, 0]
                out_ref[HALO + part * block_count : HALO + (part + 1) * block_count, :] = low_ref[
                    lines_at(at, block_count), :
                ] + delayed(high_ref, at, delay, block_count)
            out_ref[:HALO, :] = power

    pl.when(core == 0)(lambda: body(kept_ref, got_ref))
    pl.when(core == 1)(lambda: body(got_ref, kept_ref))


def pass_kernel(block_count, *refs):
    raw_refs, out_ref = refs[: len(RAW_MASKS)], refs[-1]
    power = raw_refs[0][:HALO, :]
    for ref in raw_refs[1:]:
        power = power + ref[:HALO, :]
    out_ref[:HALO, :] = power
    for number, ref in enumerate(raw_refs):
        out_ref[HALO + number * block_count : HALO + (number + 1) * block_count, :] = ref[HALO : HALO + block_count, :]


class Chip:
    def __init__(self, sizes, shifts_ref):
        self.subband_count, self.row_count, self.block_count = sizes
        self.shifts_ref = shifts_ref
        self.index = lax.axis_index("freq")
        self.core, self.chip, self.upper = self.index & 1, (self.index >> 1) & 7, self.index >> 4
        self.y, self.z, self.far = self.chip & 1, (self.chip >> 1) & 1, (self.chip >> 2) & 1

    def delays(self, level, group):
        bits = (self.core, self.y, self.z, self.far)
        node = self.subband_count - (self.subband_count >> level) + (self.upper << (3 - level)) + group
        column = bits[level] * self.row_count
        for above in range(level + 1, 4):
            column = column + (bits[above] << (4 + level - above))
        return delays_at(self.shifts_ref, node, 1, column, 2 << level)[0]


def chip_levels(sizes, shifts_ref, *refs):
    count = 1 + len(MERGED_MASKS)
    merged, raw, (passed_ref, first, second) = refs[:count], refs[count:-3], refs[-3:]
    here = Chip(sizes, shifts_ref)
    block_count = here.block_count
    power = passed_ref[:HALO, :]
    for number, (mask, ref) in enumerate(zip(RAW_MASKS, raw)):
        base = HALO + 2 * number * block_count
        own, other = here.core * block_count, (1 - here.core) * block_count
        second[lines_at(base + own, block_count), :] = ref[HALO + block_count :, :]
        at = HALO + number * block_count
        second[lines_at(base + other, block_count), :] = passed_ref[at : at + block_count, :]
        delays = here.delays(0, here.chip ^ mask)
        at = HALO + (here.chip ^ mask) * 2 * block_count
        merge(second, base, base + block_count, delays, first, at, block_count)
        power = power + ref[:HALO, :]
    for mask, ref in zip((0,) + MERGED_MASKS, merged):
        first[lines_at(HALO + (here.chip ^ mask) * 2 * block_count, 2 * block_count), :] = ref[HALO:, :]
        power = power + ref[:HALO, :]
    for level in range(1, 3):
        span = block_count << level
        for group in range(8 >> level):
            at = HALO + 2 * span * group
            merge(first, at, at + span, here.delays(level, group), second, at, block_count)
        first, second = second, first
    return functools.partial(merge, first, HALO, HALO + 8 * block_count, here.delays(3, 0)), power


def packed_levels(sizes, low_bit, bit_count, shifts_ref, msg_ref, first, second):
    subband_count, row_count, block_count = sizes
    row_bits = row_count.bit_length() - 1
    index = lax.axis_index("freq")
    power = jnp.zeros((HALO, LANES), jnp.float32)
    span = (row_count >> bit_count) * block_count
    for message in range(1 << bit_count):
        at = HALO + reversed_bits(message, bit_count) * span
        start = message * (HALO + span)
        power = power + msg_ref[start : start + HALO, :]
        first[at : at + span, :] = msg_ref[start + HALO : start + HALO + span, :]
    own = [(index >> (low_bit + k)) & 1 for k in range(bit_count)]
    source, target = first, second
    for k in range(bit_count):
        level = low_bit + k
        span = (1 << (row_bits - bit_count + k)) * block_count
        column = own[k] * row_count
        for q in range(k + 1, bit_count):
            column = column + (own[q] << (row_bits - q + k))
        groups = 1 << (bit_count - k - 1)
        node = subband_count - (subband_count >> level) + ((index >> (low_bit + bit_count)) << (bit_count - k - 1))
        delays = delays_at(shifts_ref, node, groups, column, 2 * span // block_count)
        for group in range(groups):
            at = HALO + 2 * group * span
            last = functools.partial(merge, source, at, at + span, delays[group])
            if groups > 1:
                last(target, at, block_count)
        source, target = target, source
    return last, power


def merge_kernel(sizes, levels, next_bits, shifts_ref, *refs):
    msg_refs, (out_ref, first, second, final) = refs[:-4], refs[-4:]
    _, row_count, block_count = sizes
    last, power = levels(shifts_ref, *msg_refs, first, second)
    last(final, HALO, block_count)
    span = (row_count >> next_bits) * block_count
    for message in range(1 << next_bits):
        start = message * (HALO + span)
        out_ref[start : start + HALO, :] = power
        out_ref[start + HALO : start + HALO + span, :] = final[HALO + message * span : HALO + (message + 1) * span, :]


def table_kernel(prof_ref, after_ref, table_ref):
    prof_count, tap_count = prof_ref.shape
    span_len = table_ref.shape[1]
    profiles = jnp.concatenate(
        [prof_ref[...].astype(jnp.float32), jnp.zeros((prof_count, span_len - tap_count), jnp.float32)], axis=1
    )
    for offset in range(HOLD):
        moved = profiles if offset == 0 else pltpu.roll(profiles, offset * STRIDE, 1)
        table_ref[offset * prof_count : (offset + 1) * prof_count, :] = moved.astype(jnp.bfloat16)


def final_kernel(sizes, levels, shifts_ref, table_ref, *refs):
    groups = sizes[1] * sizes[2] // GROUP
    scratch = refs[-2 * groups :]
    msg_refs, (out_ref, first, second) = refs[: -3 - 2 * groups], refs[-3 - 2 * groups : -2 * groups]
    subband_count, row_count, block_count = sizes
    prof_count = table_ref.shape[0] // HOLD
    last, power = levels(shifts_ref, *msg_refs, first, second)
    total = jnp.sum(jnp.sum(power, axis=0, keepdims=True), axis=1, keepdims=True)
    samples = subband_count * row_count * block_count * LANES
    rms_level = jnp.sqrt(subband_count * total / samples + 1e-06)
    line = lax.broadcasted_iota(jnp.int32, (block_count, LANES), 0)
    group = GROUP // block_count

    def window(number):
        final, windows = scratch[2 * number : 2 * number + 2]
        rows = range(number * group, (number + 1) * group)
        last(final, HALO - rows[0] * block_count, block_count, rows)
        for row in range(group):
            for block in range(table_ref.shape[1] // LANES):
                at = HALO + row * block_count + block
                piece = final[at : at + block_count, :]
                if block:
                    piece = jnp.where(line < block_count - block, piece, 0.0)
                windows[
                    row * block_count : (row + 1) * block_count, block * LANES : (block + 1) * LANES
                ] = piece.astype(jnp.bfloat16)

    window(0)
    for number in range(groups):
        if number + 1 < groups:
            window(number + 1)
        products = lax.dot_general(
            table_ref[...],
            scratch[2 * number + 1][...],
            (((1,), (1,)), ((), ())),
            preferred_element_type=jnp.float32,
        )
        best = products[:prof_count]
        for offset in range(1, HOLD):
            best = jnp.maximum(best, products[offset * prof_count : (offset + 1) * prof_count])
        best = best / rms_level
        for row in range(group):
            out_ref[number * group + row] = best[:, row * block_count : (row + 1) * block_count].astype(jnp.bfloat16)


def stage_groups(subband_count, low_bit, bit_count):
    groups = []
    for rest in range(subband_count >> bit_count):
        low = rest & ((1 << low_bit) - 1)
        high = rest >> low_bit
        groups.append(
            [
                low + (reversed_bits(slot, bit_count) << low_bit) + (high << (low_bit + bit_count))
                for slot in range(1 << bit_count)
            ]
        )
    return groups


def exchange(value, mask):
    return lax.ppermute(value, "freq", [(source, source ^ mask) for source in range(lax.axis_size("freq"))])


def call(kernel, out_shape, args, scratch=(), space=pltpu.VMEM):
    vmem = pl.BlockSpec(memory_space=pltpu.VMEM)
    return pl.pallas_call(
        kernel,
        out_shape=out_shape,
        in_specs=[pl.BlockSpec(memory_space=space)] * len(args),
        out_specs=jax.tree.map(lambda _: vmem, out_shape),
        scratch_shapes=list(scratch),
        compiler_params=pltpu.CompilerParams(vmem_limit_bytes=VMEM_LIMIT),
    )(*args)


def per_device(spectra, profiles, shifts):
    row_count, time_len = spectra.shape
    prof_count, tap_count = profiles.shape
    subband_count = lax.axis_size("freq")
    level_count = subband_count.bit_length() - 1
    row_bits = row_count.bit_length() - 1
    block_count = time_len // LANES
    sizes = (subband_count, row_count, block_count)
    stages = []
    while sum(stages) < level_count:
        stages.append(min(row_bits, level_count - sum(stages)))
    spectra = pltpu.with_memory_space_constraint(spectra, pltpu.HBM)
    states = [pltpu.VMEM((row_count * block_count + 2 * HALO, LANES), jnp.float32)] * 2
    fetch = [
        pltpu.VMEM(spectra.shape, jnp.float32),
        pltpu.SemaphoreType.DMA((FETCHES * row_count // 8,)),
    ]

    def lines(rows, tiles=1):
        return jax.ShapeDtypeStruct((rows * block_count + tiles * HALO, LANES), jnp.float32)

    def all_to_all(messages, low_bit, bit_count):
        shape = messages.shape
        pieces = messages.reshape(1 << bit_count, -1, LANES)
        groups = stage_groups(subband_count, low_bit, bit_count)
        return lax.all_to_all(pieces, "freq", 0, 0, tiled=True, axis_index_groups=groups).reshape(shape)

    if stages[0] == 4 and row_count == 16:
        half = row_count // 2
        *raw, sent, kept = call(
            split_kernel,
            [lines(2)] * len(RAW_MASKS) + [lines(half, half + 1)] * 2,
            (spectra,),
            fetch,
            pltpu.HBM,
        )
        raw = {mask: exchange(value, 2 * mask) for mask, value in zip(RAW_MASKS, raw)}
        got = exchange(sent, 1)
        own, *merged = call(
            functools.partial(core_merge_kernel, block_count, row_count),
            [lines(2)] * (1 + len(MERGED_MASKS)),
            (shifts, got, kept),
        )
        merged = {mask: exchange(value, 2 * mask) for mask, value in zip(MERGED_MASKS, merged)}
        passed = call(
            functools.partial(pass_kernel, block_count),
            lines(len(RAW_MASKS)),
            (*raw.values(), merged[PASS_AFTER]),
        )
        passed = exchange(passed, 1)
        after = own
        messages = [own, *merged.values(), *raw.values(), passed]
        levels = functools.partial(chip_levels, sizes)
    else:
        packed = call(pack_kernel, lines(row_count, 1 << stages[0]), (spectra,), fetch, pltpu.HBM)
        after = packed
        messages = [all_to_all(packed, 0, stages[0])]
        levels = functools.partial(packed_levels, sizes, 0, stages[0])
    low_bit = 0
    for bit_count, next_bits in zip(stages[:-1], stages[1:]):
        packed = call(
            functools.partial(merge_kernel, sizes, levels, next_bits),
            lines(row_count, 1 << next_bits),
            (shifts, *messages),
            states + states[:1],
        )
        low_bit += bit_count
        messages = [all_to_all(packed, low_bit, next_bits)]
        levels = functools.partial(packed_levels, sizes, low_bit, next_bits)
    block_len = STRIDE * HOLD
    extra = (tap_count + block_len - STRIDE - 1) // block_len
    span_len = (extra + 1) * block_len
    table = call(table_kernel, jax.ShapeDtypeStruct((HOLD * prof_count, span_len), jnp.bfloat16), (profiles, after))
    return call(
        functools.partial(final_kernel, sizes, levels),
        jax.ShapeDtypeStruct((row_count, prof_count, block_count), jnp.bfloat16),
        (shifts, table, *messages),
        states
        + [
            pltpu.VMEM((GROUP + 2 * HALO, LANES), jnp.float32),
            pltpu.VMEM((GROUP, span_len), jnp.bfloat16),
        ]
        * (row_count * block_count // GROUP),
    )


def solution(mesh):
    in_specs = (P(("beam", "freq"), None), P(), P())
    out_specs = P(("beam", "freq"), None, None)
    return jax.shard_map(
        per_device, mesh=mesh, in_specs=in_specs, out_specs=out_specs, check_vma=False
    )
```

```python
import functools

import jax
import jax.numpy as jnp
from jax import lax
from jax.experimental import pallas as pl
from jax.experimental.pallas import tpu as pltpu
from jax.sharding import PartitionSpec as P

STRIDE = 8
HOLD = 16
LANES = 128
HALO = 8
GROUP = 256
VMEM_LIMIT = 48 * 1024 * 1024
FETCHES = 4
RAW_MASKS = (7, 5)
NEAR_LINES = 7
FAR_MASKS = (4, 6)
NEAR_MASKS = (3, 2, 1)
MERGED_MASKS = FAR_MASKS + NEAR_MASKS
PASS_AFTER = 3


def reversed_bits(value, count):
    result = 0
    for bit in range(count):
        result |= ((value >> bit) & 1) << (count - 1 - bit)
    return result


def lines_at(start, count):
    if isinstance(start, int):
        return slice(start, start + count)
    return pl.ds(pl.multiple_of(start, 8), count)


def aligned_rows(x_ref, buffer, sems, store):
    row_count, time_len = x_ref.shape
    width = time_len // FETCHES
    copies = []
    for part in range(FETCHES):
        for half in range(row_count // 8):
            at = (pl.ds(half * 8, 8), pl.ds(part * width, width))
            copies.append(pltpu.make_async_copy(x_ref.at[at], buffer.at[at], sems.at[len(copies)]))
    for copy in copies:
        copy.start()
    power = jnp.zeros((8, LANES), jnp.float32)
    for part in range(FETCHES):
        for half in range(row_count // 8):
            copies[part * (row_count // 8) + half].wait()
            for column in range(part * width // LANES, (part + 1) * width // LANES):
                piece = buffer[half * 8 : half * 8 + 8, column * LANES : (column + 1) * LANES]
                power = power + piece * piece
                store(half, column, piece)
    return power


def pack_kernel(x_ref, msg_ref, buffer, sems):
    row_count, time_len = x_ref.shape
    block_count = time_len // LANES
    stride = HALO + block_count

    def store(half, column, piece):
        msg_ref[pl.ds(half * 8 * stride + HALO + column, 8, stride=stride), :] = piece

    power = aligned_rows(x_ref, buffer, sems, store)
    for row in range(row_count):
        msg_ref[row * stride : row * stride + HALO, :] = power


def split_kernel(x_ref, *refs):
    raw_refs, (sent_ref, kept_ref, buffer, sems) = refs[:-4], refs[-4:]
    index = lax.axis_index("freq")
    core, chip = index & 1, (index >> 1) & 7
    row_count, time_len = x_ref.shape
    block_count = time_len // LANES
    stride = block_count + HALO

    def body(own_half):
        def store(half, column, piece):
            ref = kept_ref if half == own_half else sent_ref
            ref[pl.ds(HALO + column, 8, stride=stride), :] = piece

        power = aligned_rows(x_ref, buffer, sems, store)
        for mask, out_ref in zip(RAW_MASKS, raw_refs):
            at = HALO + reversed_bits(chip ^ mask, 3) * stride
            out_ref[:HALO, :] = power
            out_ref[HALO : HALO + block_count, :] = sent_ref[lines_at(at, block_count), :]
            out_ref[HALO + block_count :, :] = kept_ref[lines_at(at, block_count), :]
        for ref in (sent_ref, kept_ref):
            ref[:HALO, :] = power

    for own_half in range(2):
        pl.when(core == own_half)(functools.partial(body, own_half))


def delays_at(shifts_ref, node, groups, column, count):
    rows = shifts_ref[pl.ds(node, groups), :]
    rows = jnp.concatenate([rows, jnp.zeros((groups, LANES - rows.shape[1]), jnp.int32)], axis=1)
    rows = pltpu.roll(rows, (LANES - column) & (LANES - 1), 1)
    return [[rows[group, row] for row in range(count)] for group in range(groups)]


def delayed(source, high, delay, block_count):
    lane = lax.broadcasted_iota(jnp.int32, (block_count, LANES), 1)
    line = lax.broadcasted_iota(jnp.int32, (HALO, LANES), 0)
    lines, part = delay >> 7, delay & (LANES - 1)
    near = source[pl.ds(high - lines, block_count), :]
    far = source[pl.ds(high - lines - 1, block_count), :]
    moved = pltpu.roll(jnp.where(lane < LANES - part, near, far), part, 1)
    head = jnp.where(line * LANES + lane[:HALO] >= delay, moved[:HALO], 0.0)
    return jnp.concatenate([head, moved[HALO:]], axis=0)


def merge(source, low, high, delays, target, at, block_count, rows=None):
    for row in range(len(delays)) if rows is None else rows:
        skip = row // 2 * block_count
        target[lines_at(at + row * block_count, block_count), :] = source[
            lines_at(low + skip, block_count), :
        ] + delayed(source, high + skip, delays[row], block_count)


def core_merge_kernel(block_count, row_count, shifts_ref, got_ref, kept_ref, *outs):
    index = lax.axis_index("freq")
    core, chip = index & 1, (index >> 1) & 7
    row = jnp.broadcast_to(shifts_ref[pl.ds(index >> 1, 1), :], (row_count, 2 * row_count))
    entry = lax.broadcasted_iota(jnp.int32, row.shape, 0) ^ (2 * reversed_bits(chip, 3))
    column = lax.broadcasted_iota(jnp.int32, row.shape, 1)
    picked = jnp.where(column == entry + core * row_count, row.astype(jnp.float32), 0.0)
    picked = jnp.sum(picked, axis=1, keepdims=True).astype(jnp.int32)

    def body(low_ref, high_ref):
        power = low_ref[:HALO, :] + high_ref[:HALO, :]
        for mask, out_ref in zip((0,) + MERGED_MASKS, outs):
            at = HALO + reversed_bits(chip ^ mask, 3) * (block_count + HALO)
            for part in range(2):
                delay = picked[2 * reversed_bits(mask, 3) + part, 0]
                start = part * block_count + (HALO if mask in FAR_MASKS else 0)
                out_ref[start : start + block_count, :] = low_ref[lines_at(at, block_count), :] + delayed(
                    high_ref, at, delay, block_count
                )
            if mask in FAR_MASKS:
                out_ref[:HALO, :] = power
            else:
                out_ref[2 * block_count :, :] = jnp.broadcast_to(jnp.sum(power, axis=0, keepdims=True), (NEAR_LINES, LANES))

    pl.when(core == 0)(lambda: body(kept_ref, got_ref))
    pl.when(core == 1)(lambda: body(got_ref, kept_ref))


def pass_kernel(block_count, *refs):
    raw_refs, out_ref = refs[: len(RAW_MASKS)], refs[-1]
    power = raw_refs[0][:HALO, :]
    for ref in raw_refs[1:]:
        power = power + ref[:HALO, :]
    for number, ref in enumerate(raw_refs):
        out_ref[number * block_count : (number + 1) * block_count, :] = ref[HALO : HALO + block_count, :]
    end = len(raw_refs) * block_count
    out_ref[end:, :] = jnp.broadcast_to(jnp.sum(power, axis=0, keepdims=True), (NEAR_LINES, LANES))


class Chip:
    def __init__(self, sizes, shifts_ref):
        self.subband_count, self.row_count, self.block_count = sizes
        self.shifts_ref = shifts_ref
        self.index = lax.axis_index("freq")
        self.core, self.chip, self.upper = self.index & 1, (self.index >> 1) & 7, self.index >> 4
        self.y, self.z, self.far = self.chip & 1, (self.chip >> 1) & 1, (self.chip >> 2) & 1

    def delays(self, level, group):
        bits = (self.core, self.y, self.z, self.far)
        node = self.subband_count - (self.subband_count >> level) + (self.upper << (3 - level)) + group
        column = bits[level] * self.row_count
        for above in range(level + 1, 4):
            column = column + (bits[above] << (4 + level - above))
        return delays_at(self.shifts_ref, node, 1, column, 2 << level)[0]


def near_kernel(sizes, shifts_ref, *refs):
    near, (out_ref, first, second) = refs[:4], refs[4:]
    here = Chip(sizes, shifts_ref)
    block_count = here.block_count
    span = 2 * block_count
    power = near[0][span : span + 1, :]
    for ref in near[1:]:
        power = power + ref[span : span + 1, :]
    line = lax.broadcasted_iota(jnp.int32, (HALO, LANES), 0)
    out_ref[:HALO, :] = jnp.where(line == 0, jnp.broadcast_to(power, (HALO, LANES)), 0.0)
    for mask, ref in zip((0,) + NEAR_MASKS, near):
        first[lines_at(HALO + ((here.chip ^ mask) & 3) * span, span), :] = ref[:span, :]
    for pair in range(2):
        at = HALO + 2 * pair * span
        merge(first, at, at + span, here.delays(1, 2 * here.far + pair), second, at, block_count)
    merge(second, HALO, HALO + 2 * span, here.delays(2, here.far), out_ref, HALO, block_count)


def chip_levels(sizes, shifts_ref, near_ref, *refs):
    merged, raw, (passed_ref, first, second) = refs[: len(FAR_MASKS)], refs[len(FAR_MASKS) : -3], refs[-3:]
    here = Chip(sizes, shifts_ref)
    block_count = here.block_count
    span = 2 * block_count
    line = lax.broadcasted_iota(jnp.int32, (HALO, LANES), 0)
    end = len(RAW_MASKS) * block_count
    passed_power = jnp.broadcast_to(passed_ref[end : end + 1, :], (HALO, LANES))
    power = near_ref[:HALO, :] + jnp.where(line == 0, passed_power, 0.0)
    for number, (mask, ref) in enumerate(zip(RAW_MASKS, raw)):
        base = HALO + number * span
        own, other = here.core * block_count, (1 - here.core) * block_count
        second[lines_at(base + own, block_count), :] = ref[HALO + block_count :, :]
        at = number * block_count
        second[lines_at(base + other, block_count), :] = passed_ref[at : at + block_count, :]
        at = HALO + ((here.chip ^ mask) & 3) * span
        merge(second, base, base + block_count, here.delays(0, here.chip ^ mask), first, at, block_count)
        power = power + ref[:HALO, :]
    for mask, ref in zip(FAR_MASKS, merged):
        first[lines_at(HALO + ((here.chip ^ mask) & 3) * span, span), :] = ref[HALO:, :]
        power = power + ref[:HALO, :]
    far = 1 - here.far
    for pair in range(2):
        at = HALO + 2 * pair * span
        merge(first, at, at + span, here.delays(1, 2 * far + pair), second, at, block_count)
    merge(second, HALO, HALO + 2 * span, here.delays(2, far), first, HALO + far * 4 * span, block_count)
    first[lines_at(HALO + here.far * 4 * span, 4 * span), :] = near_ref[HALO:, :]
    return functools.partial(merge, first, HALO, HALO + 4 * span, here.delays(3, 0)), power


def packed_levels(sizes, low_bit, bit_count, shifts_ref, msg_ref, first, second):
    subband_count, row_count, block_count = sizes
    row_bits = row_count.bit_length() - 1
    index = lax.axis_index("freq")
    power = jnp.zeros((HALO, LANES), jnp.float32)
    span = (row_count >> bit_count) * block_count
    for message in range(1 << bit_count):
        at = HALO + reversed_bits(message, bit_count) * span
        start = message * (HALO + span)
        power = power + msg_ref[start : start + HALO, :]
        first[at : at + span, :] = msg_ref[start + HALO : start + HALO + span, :]
    own = [(index >> (low_bit + k)) & 1 for k in range(bit_count)]
    source, target = first, second
    for k in range(bit_count):
        level = low_bit + k
        span = (1 << (row_bits - bit_count + k)) * block_count
        column = own[k] * row_count
        for q in range(k + 1, bit_count):
            column = column + (own[q] << (row_bits - q + k))
        groups = 1 << (bit_count - k - 1)
        node = subband_count - (subband_count >> level) + ((index >> (low_bit + bit_count)) << (bit_count - k - 1))
        delays = delays_at(shifts_ref, node, groups, column, 2 * span // block_count)
        for group in range(groups):
            at = HALO + 2 * group * span
            last = functools.partial(merge, source, at, at + span, delays[group])
            if groups > 1:
                last(target, at, block_count)
        source, target = target, source
    return last, power


def merge_kernel(sizes, levels, next_bits, shifts_ref, *refs):
    msg_refs, (out_ref, first, second, final) = refs[:-4], refs[-4:]
    _, row_count, block_count = sizes
    last, power = levels(shifts_ref, *msg_refs, first, second)
    last(final, HALO, block_count)
    span = (row_count >> next_bits) * block_count
    for message in range(1 << next_bits):
        start = message * (HALO + span)
        out_ref[start : start + HALO, :] = power
        out_ref[start + HALO : start + HALO + span, :] = final[HALO + message * span : HALO + (message + 1) * span, :]


def table_kernel(prof_ref, after_ref, table_ref):
    prof_count, tap_count = prof_ref.shape
    span_len = table_ref.shape[1]
    profiles = jnp.concatenate(
        [prof_ref[...].astype(jnp.float32), jnp.zeros((prof_count, span_len - tap_count), jnp.float32)], axis=1
    )
    for offset in range(HOLD):
        moved = profiles if offset == 0 else pltpu.roll(profiles, offset * STRIDE, 1)
        table_ref[offset * prof_count : (offset + 1) * prof_count, :] = moved.astype(jnp.bfloat16)


def final_kernel(sizes, levels, shifts_ref, table_ref, *refs):
    groups = sizes[1] * sizes[2] // GROUP
    scratch = refs[-2 * groups :]
    msg_refs, (out_ref, first, second) = refs[: -3 - 2 * groups], refs[-3 - 2 * groups : -2 * groups]
    subband_count, row_count, block_count = sizes
    prof_count = table_ref.shape[0] // HOLD
    last, power = levels(shifts_ref, *msg_refs, first, second)
    total = jnp.sum(jnp.sum(power, axis=0, keepdims=True), axis=1, keepdims=True)
    samples = subband_count * row_count * block_count * LANES
    rms_level = jnp.sqrt(subband_count * total / samples + 1e-06)
    line = lax.broadcasted_iota(jnp.int32, (block_count, LANES), 0)
    group = GROUP // block_count

    def window(number):
        final, windows = scratch[2 * number : 2 * number + 2]
        rows = range(number * group, (number + 1) * group)
        last(final, HALO - rows[0] * block_count, block_count, rows)
        for row in range(group):
            for block in range(table_ref.shape[1] // LANES):
                at = HALO + row * block_count + block
                piece = final[at : at + block_count, :]
                if block:
                    piece = jnp.where(line < block_count - block, piece, 0.0)
                windows[
                    row * block_count : (row + 1) * block_count, block * LANES : (block + 1) * LANES
                ] = piece.astype(jnp.bfloat16)

    window(0)
    for number in range(groups):
        if number + 1 < groups:
            window(number + 1)
        products = lax.dot_general(
            table_ref[...],
            scratch[2 * number + 1][...],
            (((1,), (1,)), ((), ())),
            preferred_element_type=jnp.float32,
        )
        best = products[:prof_count]
        for offset in range(1, HOLD):
            best = jnp.maximum(best, products[offset * prof_count : (offset + 1) * prof_count])
        best = best / rms_level
        for row in range(group):
            out_ref[number * group + row] = best[:, row * block_count : (row + 1) * block_count].astype(jnp.bfloat16)


def stage_groups(subband_count, low_bit, bit_count):
    groups = []
    for rest in range(subband_count >> bit_count):
        low = rest & ((1 << low_bit) - 1)
        high = rest >> low_bit
        groups.append(
            [
                low + (reversed_bits(slot, bit_count) << low_bit) + (high << (low_bit + bit_count))
                for slot in range(1 << bit_count)
            ]
        )
    return groups


def exchange(value, mask):
    return lax.ppermute(value, "freq", [(source, source ^ mask) for source in range(lax.axis_size("freq"))])


def call(kernel, out_shape, args, scratch=(), space=pltpu.VMEM):
    vmem = pl.BlockSpec(memory_space=pltpu.VMEM)
    return pl.pallas_call(
        kernel,
        out_shape=out_shape,
        in_specs=[pl.BlockSpec(memory_space=space)] * len(args),
        out_specs=jax.tree.map(lambda _: vmem, out_shape),
        scratch_shapes=list(scratch),
        compiler_params=pltpu.CompilerParams(vmem_limit_bytes=VMEM_LIMIT),
    )(*args)


def per_device(spectra, profiles, shifts):
    row_count, time_len = spectra.shape
    prof_count, tap_count = profiles.shape
    subband_count = lax.axis_size("freq")
    level_count = subband_count.bit_length() - 1
    row_bits = row_count.bit_length() - 1
    block_count = time_len // LANES
    sizes = (subband_count, row_count, block_count)
    stages = []
    while sum(stages) < level_count:
        stages.append(min(row_bits, level_count - sum(stages)))
    spectra = pltpu.with_memory_space_constraint(spectra, pltpu.HBM)
    states = [pltpu.VMEM((row_count * block_count + 2 * HALO, LANES), jnp.float32)] * 2
    fetch = [
        pltpu.VMEM(spectra.shape, jnp.float32),
        pltpu.SemaphoreType.DMA((FETCHES * row_count // 8,)),
    ]

    def lines(rows, tiles=1):
        return jax.ShapeDtypeStruct((rows * block_count + tiles * HALO, LANES), jnp.float32)

    def all_to_all(messages, low_bit, bit_count):
        shape = messages.shape
        pieces = messages.reshape(1 << bit_count, -1, LANES)
        groups = stage_groups(subband_count, low_bit, bit_count)
        return lax.all_to_all(pieces, "freq", 0, 0, tiled=True, axis_index_groups=groups).reshape(shape)

    if stages[0] == 4 and row_count == 16:
        half = row_count // 2
        near_shape = jax.ShapeDtypeStruct((2 * block_count + NEAR_LINES, LANES), jnp.float32)
        *raw, sent, kept = call(
            split_kernel,
            [lines(2)] * len(RAW_MASKS) + [lines(half, half + 1)] * 2,
            (spectra,),
            fetch,
            pltpu.HBM,
        )
        raw = {mask: exchange(value, 2 * mask) for mask, value in zip(RAW_MASKS, raw)}
        got = exchange(sent, 1)
        own, *merged = call(
            functools.partial(core_merge_kernel, block_count, row_count),
            [near_shape] + [lines(2) if mask in FAR_MASKS else near_shape for mask in MERGED_MASKS],
            (shifts, got, kept),
        )
        merged = {mask: exchange(value, 2 * mask) for mask, value in zip(MERGED_MASKS, merged)}
        passed = call(
            functools.partial(pass_kernel, block_count),
            near_shape,
            (*raw.values(), merged[PASS_AFTER]),
        )
        passed = exchange(passed, 1)
        after = own
        near = call(
            functools.partial(near_kernel, sizes),
            lines(half),
            (shifts, own, *(merged[mask] for mask in NEAR_MASKS)),
            states,
        )
        messages = [near, *(merged[mask] for mask in FAR_MASKS), *raw.values(), passed]
        levels = functools.partial(chip_levels, sizes)
    else:
        packed = call(pack_kernel, lines(row_count, 1 << stages[0]), (spectra,), fetch, pltpu.HBM)
        after = packed
        messages = [all_to_all(packed, 0, stages[0])]
        levels = functools.partial(packed_levels, sizes, 0, stages[0])
    low_bit = 0
    for bit_count, next_bits in zip(stages[:-1], stages[1:]):
        packed = call(
            functools.partial(merge_kernel, sizes, levels, next_bits),
            lines(row_count, 1 << next_bits),
            (shifts, *messages),
            states + states[:1],
        )
        low_bit += bit_count
        messages = [all_to_all(packed, low_bit, next_bits)]
        levels = functools.partial(packed_levels, sizes, low_bit, next_bits)
    block_len = STRIDE * HOLD
    extra = (tap_count + block_len - STRIDE - 1) // block_len
    span_len = (extra + 1) * block_len
    table = call(table_kernel, jax.ShapeDtypeStruct((HOLD * prof_count, span_len), jnp.bfloat16), (profiles, after))
    return call(
        functools.partial(final_kernel, sizes, levels),
        jax.ShapeDtypeStruct((row_count, prof_count, block_count), jnp.bfloat16),
        (shifts, table, *messages),
        states
        + [
            pltpu.VMEM((GROUP + 2 * HALO, LANES), jnp.float32),
            pltpu.VMEM((GROUP, span_len), jnp.bfloat16),
        ]
        * (row_count * block_count // GROUP),
    )


def solution(mesh):
    in_specs = (P(("beam", "freq"), None), P(), P())
    out_specs = P(("beam", "freq"), None, None)
    return jax.shard_map(
        per_device, mesh=mesh, in_specs=in_specs, out_specs=out_specs, check_vma=False
    )
```

```python
import functools

import jax
import jax.numpy as jnp
from jax import lax
from jax.experimental import pallas as pl
from jax.experimental.pallas import tpu as pltpu
from jax.sharding import PartitionSpec as P

STRIDE = 8
HOLD = 16
LANES = 128
HALO = 8
VMEM_LIMIT = 48 * 1024 * 1024
FETCHES = 4
RAW_MASKS = (7, 5)
MERGED_MASKS = (4, 6, 3, 2, 1)
PASS_AFTER = 3


def reversed_bits(value, count):
    result = 0
    for bit in range(count):
        result |= ((value >> bit) & 1) << (count - 1 - bit)
    return result


def lines_at(start, count):
    if isinstance(start, int):
        return slice(start, start + count)
    return pl.ds(pl.multiple_of(start, 8), count)


def aligned_rows(x_ref, buffer, sems, store):
    row_count, time_len = x_ref.shape
    width = time_len // FETCHES
    copies = []
    for part in range(FETCHES):
        for half in range(row_count // 8):
            at = (pl.ds(half * 8, 8), pl.ds(part * width, width))
            copies.append(pltpu.make_async_copy(x_ref.at[at], buffer.at[at], sems.at[len(copies)]))
    for copy in copies:
        copy.start()
    power = jnp.zeros((8, LANES), jnp.float32)
    for part in range(FETCHES):
        for half in range(row_count // 8):
            copies[part * (row_count // 8) + half].wait()
            for column in range(part * width // LANES, (part + 1) * width // LANES):
                piece = buffer[half * 8 : half * 8 + 8, column * LANES : (column + 1) * LANES]
                power = power + piece * piece
                store(half, column, piece)
    return power


def pack_kernel(x_ref, msg_ref, buffer, sems):
    row_count, time_len = x_ref.shape
    block_count = time_len // LANES
    stride = HALO + block_count

    def store(half, column, piece):
        msg_ref[pl.ds(half * 8 * stride + HALO + column, 8, stride=stride), :] = piece

    power = aligned_rows(x_ref, buffer, sems, store)
    for row in range(row_count):
        msg_ref[row * stride : row * stride + HALO, :] = power


def split_kernel(x_ref, *refs):
    raw_refs, (sent_ref, kept_ref, rows, buffer, sems) = refs[:-5], refs[-5:]
    index = lax.axis_index("freq")
    core, chip = index & 1, (index >> 1) & 7
    row_count, time_len = x_ref.shape
    block_count = time_len // LANES
    half_rows = row_count // 2
    stride = block_count + HALO

    def store(half, column, piece):
        rows[pl.ds(half * 8 * stride + column, 8, stride=stride), :] = piece

    power = aligned_rows(x_ref, buffer, sems, store)
    for ref in (*raw_refs, sent_ref, kept_ref):
        ref[:HALO, :] = power
    sent_at, kept_at = (1 - core) * half_rows * stride, core * half_rows * stride
    for mask, out_ref in zip(RAW_MASKS, raw_refs):
        at = reversed_bits(chip ^ mask, 3) * stride
        out_ref[HALO : HALO + block_count, :] = rows[lines_at(sent_at + at, block_count), :]
        out_ref[HALO + block_count :, :] = rows[lines_at(kept_at + at, block_count), :]
    for row in range(half_rows):
        for ref, at in ((sent_ref, sent_at), (kept_ref, kept_at)):
            ref[HALO + row * block_count : HALO + (row + 1) * block_count, :] = rows[
                lines_at(at + row * stride, block_count), :
            ]


def delays_at(shifts_ref, node, groups, column, count):
    rows = shifts_ref[pl.ds(node, groups), :]
    rows = jnp.concatenate([rows, jnp.zeros((groups, LANES - rows.shape[1]), jnp.int32)], axis=1)
    rows = pltpu.roll(rows, (LANES - column) & (LANES - 1), 1)
    return [[rows[group, row] for row in range(count)] for group in range(groups)]


def delayed(source, high, delay, block_count):
    lane = lax.broadcasted_iota(jnp.int32, (block_count, LANES), 1)
    line = lax.broadcasted_iota(jnp.int32, (HALO, LANES), 0)
    lines, part = delay >> 7, delay & (LANES - 1)
    near = source[pl.ds(high - lines, block_count), :]
    far = source[pl.ds(high - lines - 1, block_count), :]
    moved = pltpu.roll(jnp.where(lane < LANES - part, near, far), part, 1)
    head = jnp.where(line * LANES + lane[:HALO] >= delay, moved[:HALO], 0.0)
    return jnp.concatenate([head, moved[HALO:]], axis=0)


def merge(source, low, high, delays, target, at, block_count, rows=None):
    for row in range(len(delays)) if rows is None else rows:
        skip = row // 2 * block_count
        target[lines_at(at + row * block_count, block_count), :] = source[
            lines_at(low + skip, block_count), :
        ] + delayed(source, high + skip, delays[row], block_count)


def core_merge_kernel(block_count, row_count, shifts_ref, got_ref, kept_ref, *outs):
    index = lax.axis_index("freq")
    core, chip = index & 1, (index >> 1) & 7
    row = jnp.broadcast_to(shifts_ref[pl.ds(index >> 1, 1), :], (row_count, 2 * row_count))
    entry = lax.broadcasted_iota(jnp.int32, row.shape, 0) ^ (2 * reversed_bits(chip, 3))
    column = lax.broadcasted_iota(jnp.int32, row.shape, 1)
    picked = jnp.where(column == entry + core * row_count, row.astype(jnp.float32), 0.0)
    picked = jnp.sum(picked, axis=1, keepdims=True).astype(jnp.int32)

    def body(low_ref, high_ref):
        power = low_ref[:HALO, :] + high_ref[:HALO, :]
        for mask, out_ref in zip((0,) + MERGED_MASKS, outs):
            at = HALO + reversed_bits(chip ^ mask, 3) * block_count
            for part in range(2):
                delay = picked[2 * reversed_bits(mask, 3) + part, 0]
                out_ref[HALO + part * block_count : HALO + (part + 1) * block_count, :] = low_ref[
                    lines_at(at, block_count), :
                ] + delayed(high_ref, at, delay, block_count)
            out_ref[:HALO, :] = power

    pl.when(core == 0)(lambda: body(kept_ref, got_ref))
    pl.when(core == 1)(lambda: body(got_ref, kept_ref))


def pass_kernel(block_count, *refs):
    raw_refs, out_ref = refs[: len(RAW_MASKS)], refs[-1]
    power = raw_refs[0][:HALO, :]
    for ref in raw_refs[1:]:
        power = power + ref[:HALO, :]
    out_ref[:HALO, :] = power
    for number, ref in enumerate(raw_refs):
        out_ref[HALO + number * block_count : HALO + (number + 1) * block_count, :] = ref[HALO : HALO + block_count, :]


class Chip:
    def __init__(self, sizes, shifts_ref):
        self.subband_count, self.row_count, self.block_count = sizes
        self.shifts_ref = shifts_ref
        self.index = lax.axis_index("freq")
        self.core, self.chip, self.upper = self.index & 1, (self.index >> 1) & 7, self.index >> 4
        self.y, self.z, self.far = self.chip & 1, (self.chip >> 1) & 1, (self.chip >> 2) & 1

    def delays(self, level, group):
        bits = (self.core, self.y, self.z, self.far)
        node = self.subband_count - (self.subband_count >> level) + (self.upper << (3 - level)) + group
        column = bits[level] * self.row_count
        for above in range(level + 1, 4):
            column = column + (bits[above] << (4 + level - above))
        return delays_at(self.shifts_ref, node, 1, column, 2 << level)[0]


def chip_levels(sizes, shifts_ref, *refs):
    count = 1 + len(MERGED_MASKS)
    merged, raw, (passed_ref, first, second) = refs[:count], refs[count:-3], refs[-3:]
    here = Chip(sizes, shifts_ref)
    block_count = here.block_count
    power = passed_ref[:HALO, :]
    for number, (mask, ref) in enumerate(zip(RAW_MASKS, raw)):
        base = HALO + 2 * number * block_count
        own, other = here.core * block_count, (1 - here.core) * block_count
        second[lines_at(base + own, block_count), :] = ref[HALO + block_count :, :]
        at = HALO + number * block_count
        second[lines_at(base + other, block_count), :] = passed_ref[at : at + block_count, :]
        delays = here.delays(0, here.chip ^ mask)
        at = HALO + (here.chip ^ mask) * 2 * block_count
        merge(second, base, base + block_count, delays, first, at, block_count)
        power = power + ref[:HALO, :]
    for mask, ref in zip((0,) + MERGED_MASKS, merged):
        first[lines_at(HALO + (here.chip ^ mask) * 2 * block_count, 2 * block_count), :] = ref[HALO:, :]
        power = power + ref[:HALO, :]
    for level in range(1, 3):
        span = block_count << level
        for group in range(8 >> level):
            at = HALO + 2 * span * group
            merge(first, at, at + span, here.delays(level, group), second, at, block_count)
        first, second = second, first
    last = functools.partial(merge, first, HALO, HALO + 8 * block_count, here.delays(3, 0), second, HALO, block_count)
    return last, second, power


def packed_levels(sizes, low_bit, bit_count, shifts_ref, msg_ref, first, second):
    subband_count, row_count, block_count = sizes
    row_bits = row_count.bit_length() - 1
    index = lax.axis_index("freq")
    power = jnp.zeros((HALO, LANES), jnp.float32)
    span = (row_count >> bit_count) * block_count
    for message in range(1 << bit_count):
        at = HALO + reversed_bits(message, bit_count) * span
        start = message * (HALO + span)
        power = power + msg_ref[start : start + HALO, :]
        first[at : at + span, :] = msg_ref[start + HALO : start + HALO + span, :]
    own = [(index >> (low_bit + k)) & 1 for k in range(bit_count)]
    source, target = first, second
    for k in range(bit_count):
        level = low_bit + k
        span = (1 << (row_bits - bit_count + k)) * block_count
        column = own[k] * row_count
        for q in range(k + 1, bit_count):
            column = column + (own[q] << (row_bits - q + k))
        groups = 1 << (bit_count - k - 1)
        node = subband_count - (subband_count >> level) + ((index >> (low_bit + bit_count)) << (bit_count - k - 1))
        delays = delays_at(shifts_ref, node, groups, column, 2 * span // block_count)
        for group in range(groups):
            at = HALO + 2 * group * span
            last = functools.partial(merge, source, at, at + span, delays[group], target, at, block_count)
            if groups > 1:
                last()
        source, target = target, source
    return last, source, power


def merge_kernel(sizes, levels, next_bits, shifts_ref, *refs):
    msg_refs, (out_ref, first, second) = refs[:-3], refs[-3:]
    _, row_count, block_count = sizes
    last, final, power = levels(shifts_ref, *msg_refs, first, second)
    last()
    span = (row_count >> next_bits) * block_count
    for message in range(1 << next_bits):
        start = message * (HALO + span)
        out_ref[start : start + HALO, :] = power
        out_ref[start + HALO : start + HALO + span, :] = final[HALO + message * span : HALO + (message + 1) * span, :]


def table_kernel(prof_ref, after_ref, table_ref):
    prof_count, tap_count = prof_ref.shape
    span_len = table_ref.shape[1]
    profiles = jnp.concatenate(
        [prof_ref[...].astype(jnp.float32), jnp.zeros((prof_count, span_len - tap_count), jnp.float32)], axis=1
    )
    for offset in range(HOLD):
        moved = profiles if offset == 0 else pltpu.roll(profiles, offset * STRIDE, 1)
        table_ref[offset * prof_count : (offset + 1) * prof_count, :] = moved.astype(jnp.bfloat16)


def final_kernel(sizes, levels, shifts_ref, table_ref, *refs):
    msg_refs, (out_ref, first, second, windows) = refs[:-4], refs[-4:]
    subband_count, row_count, block_count = sizes
    prof_count = table_ref.shape[0] // HOLD
    last, final, power = levels(shifts_ref, *msg_refs, first, second)
    total = jnp.sum(jnp.sum(power, axis=0, keepdims=True), axis=1, keepdims=True)
    samples = subband_count * row_count * block_count * LANES
    rms_level = jnp.sqrt(subband_count * total / samples + 1e-06)
    line = lax.broadcasted_iota(jnp.int32, (block_count, LANES), 0)
    group = 256 // block_count
    for start in range(0, row_count, group):
        last(rows=range(start, start + group))
        for row in range(start, start + group):
            for block in range(table_ref.shape[1] // LANES):
                at = HALO + row * block_count + block
                piece = final[at : at + block_count, :]
                if block:
                    piece = jnp.where(line < block_count - block, piece, 0.0)
                windows[
                    row * block_count : (row + 1) * block_count, block * LANES : (block + 1) * LANES
                ] = piece.astype(jnp.bfloat16)
        products = lax.dot_general(
            table_ref[...],
            windows[start * block_count : (start + group) * block_count, :],
            (((1,), (1,)), ((), ())),
            preferred_element_type=jnp.float32,
        )
        best = products[:prof_count]
        for offset in range(1, HOLD):
            best = jnp.maximum(best, products[offset * prof_count : (offset + 1) * prof_count])
        best = best / rms_level
        for row in range(group):
            out_ref[start + row] = best[:, row * block_count : (row + 1) * block_count].astype(jnp.bfloat16)


def stage_groups(subband_count, low_bit, bit_count):
    groups = []
    for rest in range(subband_count >> bit_count):
        low = rest & ((1 << low_bit) - 1)
        high = rest >> low_bit
        groups.append(
            [
                low + (reversed_bits(slot, bit_count) << low_bit) + (high << (low_bit + bit_count))
                for slot in range(1 << bit_count)
            ]
        )
    return groups


def exchange(value, mask):
    return lax.ppermute(value, "freq", [(source, source ^ mask) for source in range(lax.axis_size("freq"))])


def call(kernel, out_shape, args, scratch=(), space=pltpu.VMEM):
    vmem = pl.BlockSpec(memory_space=pltpu.VMEM)
    return pl.pallas_call(
        kernel,
        out_shape=out_shape,
        in_specs=[pl.BlockSpec(memory_space=space)] * len(args),
        out_specs=jax.tree.map(lambda _: vmem, out_shape),
        scratch_shapes=list(scratch),
        compiler_params=pltpu.CompilerParams(vmem_limit_bytes=VMEM_LIMIT),
    )(*args)


def per_device(spectra, profiles, shifts):
    row_count, time_len = spectra.shape
    prof_count, tap_count = profiles.shape
    subband_count = lax.axis_size("freq")
    level_count = subband_count.bit_length() - 1
    row_bits = row_count.bit_length() - 1
    block_count = time_len // LANES
    sizes = (subband_count, row_count, block_count)
    stages = []
    while sum(stages) < level_count:
        stages.append(min(row_bits, level_count - sum(stages)))
    spectra = pltpu.with_memory_space_constraint(spectra, pltpu.HBM)
    states = [pltpu.VMEM((row_count * block_count + 2 * HALO, LANES), jnp.float32)] * 2
    fetch = [
        pltpu.VMEM(spectra.shape, jnp.float32),
        pltpu.SemaphoreType.DMA((FETCHES * row_count // 8,)),
    ]

    def lines(rows, tiles=1):
        return jax.ShapeDtypeStruct((rows * block_count + tiles * HALO, LANES), jnp.float32)

    def all_to_all(messages, low_bit, bit_count):
        shape = messages.shape
        pieces = messages.reshape(1 << bit_count, -1, LANES)
        groups = stage_groups(subband_count, low_bit, bit_count)
        return lax.all_to_all(pieces, "freq", 0, 0, tiled=True, axis_index_groups=groups).reshape(shape)

    if stages[0] == 4 and row_count == 16:
        half = row_count // 2
        *raw, sent, kept = call(
            split_kernel,
            [lines(2)] * len(RAW_MASKS) + [lines(half)] * 2,
            (spectra,),
            [pltpu.VMEM((row_count * (block_count + HALO), LANES), jnp.float32)] + fetch,
            pltpu.HBM,
        )
        raw = {mask: exchange(value, 2 * mask) for mask, value in zip(RAW_MASKS, raw)}
        got = exchange(sent, 1)
        own, *merged = call(
            functools.partial(core_merge_kernel, block_count, row_count),
            [lines(2)] * (1 + len(MERGED_MASKS)),
            (shifts, got, kept),
        )
        merged = {mask: exchange(value, 2 * mask) for mask, value in zip(MERGED_MASKS, merged)}
        passed = call(
            functools.partial(pass_kernel, block_count),
            lines(len(RAW_MASKS)),
            (*raw.values(), merged[PASS_AFTER]),
        )
        passed = exchange(passed, 1)
        after = own
        messages = [own, *merged.values(), *raw.values(), passed]
        levels = functools.partial(chip_levels, sizes)
    else:
        packed = call(pack_kernel, lines(row_count, 1 << stages[0]), (spectra,), fetch, pltpu.HBM)
        after = packed
        messages = [all_to_all(packed, 0, stages[0])]
        levels = functools.partial(packed_levels, sizes, 0, stages[0])
    low_bit = 0
    for bit_count, next_bits in zip(stages[:-1], stages[1:]):
        packed = call(
            functools.partial(merge_kernel, sizes, levels, next_bits),
            lines(row_count, 1 << next_bits),
            (shifts, *messages),
            states,
        )
        low_bit += bit_count
        messages = [all_to_all(packed, low_bit, next_bits)]
        levels = functools.partial(packed_levels, sizes, low_bit, next_bits)
    block_len = STRIDE * HOLD
    extra = (tap_count + block_len - STRIDE - 1) // block_len
    span_len = (extra + 1) * block_len
    table = call(table_kernel, jax.ShapeDtypeStruct((HOLD * prof_count, span_len), jnp.bfloat16), (profiles, after))
    return call(
        functools.partial(final_kernel, sizes, levels),
        jax.ShapeDtypeStruct((row_count, prof_count, block_count), jnp.bfloat16),
        (shifts, table, *messages),
        states + [pltpu.VMEM((row_count * block_count, span_len), jnp.bfloat16)],
    )


def solution(mesh):
    in_specs = (P(("beam", "freq"), None), P(), P())
    out_specs = P(("beam", "freq"), None, None)
    return jax.shard_map(
        per_device, mesh=mesh, in_specs=in_specs, out_specs=out_specs, check_vma=False
    )
```
